32 devices in a mesh: depth: 4 (over z), imx: 4 (over y, x), imy: 2 (over core).
Axes of the slice: x: 2, y: 2, z: 4, core: 2. Of those that a mesh axis runs over, the one named last changes fastest.
Arguments:
- field: bfloat16 [128, 256, 512], P('depth', 'imy', 'imx'), may hold values from -6 to 6
- brick_live: int32 [4, 8, 16], P('depth', 'imy', 'imx'), may hold values from 0 to 1, as said below
- order: int32 [32, 64], P('imy', 'imx'), may hold values 0 or 1
- centers: float32 [4], replicated, may hold values from -2 to 2
- widths: float32 [4], replicated, may hold values from 0.3 to 1.2
- heights: float32 [4], replicated, may hold values from 0.5 to 3
- colours: float32 [4, 3], replicated, may hold values from 0.1 to 1
Outputs:
- colour: float32 [3, 256, 512], P(None, ('imy', 'depth'), 'imx')
- logtrans: float32 [256, 512], P(('imy', 'depth'), 'imx')
The draws below stay inside these ranges and needn't reach their ends.
Inputs may be any that keep to these rules, and one draw needn't show every extreme that they name: `brick_live`: each device's 16 bricks (one slab, 4 bricks along the rows by 4 along the columns) hold between 1 and 16 live bricks; at least one device has all 16 live, and most have few.
All inputs are finite; a program needn't handle non-finite values. No bound on the sum of `order` on one device may be relied on, other than what follows from the above.
Results may differ from the reference program's by a relative error of at most 0.00038.
Values may be sent and summed in bfloat16 or wider, within the bound.
A program may use at most 64 MiB of HBM per device.

```python
import math
import jax
import jax.numpy as jnp
from jax import lax

BRICK = 32
BX_DEV = 4
BY_DEV = 4
NB = 4
TILE = 8
Z_DEV = 32
BRICKS_DEV = 16
NZ = 128
NX = 256
NY = 512
SLABS = 4
ROW_BLOCKS = 2
COL_BLOCKS = 4


def draw_brick_live(key, part):
    keys = jax.random.split(jax.random.fold_in(key, 7177), 4)
    first = jax.random.randint(keys[0], (SLABS, ROW_BLOCKS, COL_BLOCKS), 0, 8)
    second = jax.random.randint(keys[1], (SLABS, ROW_BLOCKS, COL_BLOCKS), 0, 8)
    counts = 1 + first * second * (BRICKS_DEV - 1) // 49
    chosen = jax.random.randint(keys[2], (), 0, SLABS * ROW_BLOCKS * COL_BLOCKS)
    flat = jnp.arange(SLABS * ROW_BLOCKS * COL_BLOCKS, dtype=jnp.int32).reshape(SLABS, ROW_BLOCKS, COL_BLOCKS)
    counts = jnp.where(flat == chosen, BRICKS_DEV, counts)
    scores = jax.random.randint(keys[3], (SLABS, ROW_BLOCKS, COL_BLOCKS, BRICKS_DEV), 0, 1 << 20) * BRICKS_DEV
    scores = scores + jnp.arange(BRICKS_DEV, dtype=jnp.int32)[None, None, None, :]
    ranks = jnp.argsort(jnp.argsort(scores, axis=3, stable=True), axis=3, stable=True)
    live = (ranks < counts[:, :, :, None]).astype(jnp.int32)
    live = live.reshape(SLABS, ROW_BLOCKS, COL_BLOCKS, BX_DEV, BY_DEV)
    live = jnp.transpose(live, (0, 1, 3, 2, 4))
    return live.reshape(SLABS, ROW_BLOCKS * BX_DEV, COL_BLOCKS * BY_DEV)


def with_ends(entries, key, least, largest):
    dims = entries.shape
    index_at = [jax.random.randint(jax.random.fold_in(key, axis), (), 0, dims[axis]) for axis in range(len(dims))]
    entries = entries.at[tuple(index_at)].set(least)
    longest = dims.index(max(dims))
    index_at[longest] = (index_at[longest] + 1) % dims[longest]
    return entries.at[tuple(index_at)].set(largest)


def shard_levels(key, shape, shards, low, high):
    def one(axis_at, blocks):
        draws = jax.random.uniform(jax.random.fold_in(jax.random.fold_in(key, 6), axis_at), (blocks,), jnp.float32, low / len(shards), high / len(shards))
        return jnp.repeat(jnp.exp(draws), shape[axis_at] // blocks).reshape((-1,) + (1,) * (len(shape) - axis_at - 1))

    factor_of = one(*shards[0])
    for cut in shards[1:]:
        factor_of = factor_of * one(*cut)
    return factor_of


def noise(own_key, extent, width, bound, pieces=(), kind=jnp.bfloat16):
    loudness = shard_levels(own_key, extent, pieces, -0.22, 0.18) if pieces else 1.0
    drawn = jax.random.normal(own_key, extent, jnp.float32) * width * loudness
    return jnp.minimum(jnp.maximum(drawn, -bound), bound).astype(kind)


def setup_inputs(seed: int = 0) -> dict:
    seeds = jax.random.split(jax.random.key(seed), 8)
    return {
        "field": noise(seeds[0], (NZ, NX, NY), 1.0, 6.0, ((0, 4), (1, 2), (2, 4))),
        "brick_live": draw_brick_live(jax.random.fold_in(seeds[7], 71), 0),
        "order": with_ends((jax.random.randint(seeds[2], (NX // TILE, NY // TILE), 0, 2) < 1).astype(jnp.int32), jax.random.fold_in(seeds[2], 1), 0, 1),
        "centers": jnp.clip(jax.random.uniform(seeds[3], (NB,), jnp.float32, -2.0, 2.0), -2.0, 2.0),
        "widths": jnp.clip(jnp.exp(jax.random.uniform(seeds[4], (NB,), jnp.float32, math.log(0.3), math.log(1.2))), 0.3, 1.2),
        "heights": jnp.clip(jnp.exp(jax.random.uniform(seeds[5], (NB,), jnp.float32, math.log(0.5), math.log(3.0))), 0.5, 3.0),
        "colours": jnp.clip(jax.random.uniform(seeds[6], (NB, 3), jnp.float32, 0.1, 1.0), 0.1, 1.0),
    }


OPTICAL = 3.0

def shade_cells(padded):
    grad_z = (padded[2:, 1:-1, 1:-1] - padded[:-2, 1:-1, 1:-1]) * 0.5
    grad_x = (padded[1:-1, 2:, 1:-1] - padded[1:-1, :-2, 1:-1]) * 0.5
    grad_y = (padded[1:-1, 1:-1, 2:] - padded[1:-1, 1:-1, :-2]) * 0.5
    facing = grad_z * 0.64 + grad_x * 0.48 + grad_y * 0.6
    length = lax.rsqrt(grad_z * grad_z + grad_x * grad_x + grad_y * grad_y + 1.0)
    return (0.3 + 0.7 * jnp.abs(facing) * length).astype(jnp.bfloat16)

def render_cells(values, shade, backward, live, centers, widths, heights, colours, step_len):
    valf = values.astype(jnp.float32)
    sigma = jnp.zeros(valf.shape, jnp.float32)
    emits = [jnp.zeros(valf.shape, jnp.float32) for chan in range(3)]
    for bumpno in range(centers.shape[0]):
        bump = jnp.exp(-0.5 * jnp.square((valf - centers[bumpno]) / widths[bumpno]))
        sigma = sigma + heights[bumpno] * bump
        emits = [emits[chan] + colours[bumpno, chan] * bump for chan in range(3)]
    tau = sigma * (step_len * live)
    absorb = -jnp.expm1(-tau)
    running = jnp.cumsum(tau, axis=0)
    total = running[-1]
    before = jnp.where(backward, total - running, running - tau)
    weight = jnp.exp(-before) * absorb * shade.astype(jnp.float32)
    parts = [lax.optimization_barrier(jnp.sum(weight * emits[chan], axis=0)) for chan in range(3)]
    return jnp.stack(parts + [-total])

def reference(field, brick_live, order, centers, widths, heights, colours):
    step_len = OPTICAL / NZ
    padded = jnp.pad(field, 1)
    backward = jnp.repeat(jnp.repeat(order, TILE, axis=0), TILE, axis=1) == 1

    def one_slab(slab):
        block = lax.dynamic_slice(padded, (slab * Z_DEV, jnp.int32(0), jnp.int32(0)), (Z_DEV + 2, NX + 2, NY + 2)).astype(jnp.float32)
        shade = shade_cells(block)
        live_here = lax.dynamic_index_in_dim(brick_live, slab, 0, keepdims=False)
        live = jnp.repeat(jnp.repeat(live_here, BRICK, axis=0), BRICK, axis=1).astype(jnp.float32)
        return render_cells(block[1:-1, 1:-1, 1:-1], shade, backward, live, centers, widths, heights, colours, step_len)
    tiles = lax.map(one_slab, jnp.arange(SLABS, dtype=jnp.int32))

    def over(carry, tile):
        colour_acc, logt_acc = carry
        return ((colour_acc + jnp.exp(logt_acc) * tile[:3], logt_acc + tile[3]), None)
    start = (jnp.zeros((3, NX, NY), jnp.float32), jnp.zeros((NX, NY), jnp.float32))
    forward, unused = lax.scan(over, start, tiles)
    reverse_pass, unused = lax.scan(over, start, tiles, reverse=True)
    colour = jnp.where(backward, reverse_pass[0], forward[0])
    logtrans = jnp.where(backward, reverse_pass[1], forward[1])
    return (colour, logtrans)
```

```python
import functools
import math

import jax
import jax.numpy as jnp
from jax import lax
from jax.experimental import pallas as pl
from jax.experimental.pallas import tpu as pltpu
from jax.sharding import PartitionSpec as P

OPTICAL = 3.0
MESH = pl.DeviceIdType.MESH
SUB = 8
PACK = 16
F32 = jnp.float32
BF16 = jnp.bfloat16
LEVELS = 32000.0
UNROLL_A = 16
CHUNK = 16
PIECES = 4
LOG2E = math.log2(math.e)


def iota(shape, dim):
    return lax.broadcasted_iota(jnp.int32, shape, dim)


def expand(small, rows, cols):
    high, wide = small.shape
    down = (iota((rows, high), 0) // (rows // high) == iota((rows, high), 1)).astype(F32).astype(BF16)
    along = (iota((wide, cols), 1) // (cols // wide) == iota((wide, cols), 0)).astype(F32).astype(BF16)
    tall = jnp.dot(down, small.astype(F32).astype(BF16), preferred_element_type=F32)
    return jnp.dot(tall.astype(BF16), along, preferred_element_type=F32)


def kernel(
    counts, step_len,
    field, live_in, order_in, centers_in, widths_in, heights_in, colours_in,
    colour_out, logt_out,
    fb, live, order, centers, widths, heights, colours,
    vf, zlo, zhi, xlo, xhi, face, flo, fhi, edges, slopes, weights, lobes, scales, flag, logs, logs_in,
    tiles_out, tiles_in, stage, own, peaks_out, peaks_in,
    load_sem, piece_sem, halo_send, halo_recv, log_send, log_recv, tile_send, tile_recv, peak_send, peak_recv,
):
    ndepth, nimx, nimy = counts
    me = lax.axis_index("depth")
    mx = lax.axis_index("imx")
    my = lax.axis_index("imy")
    zdev, xdev, ydev = fb.shape
    rows_out = xdev // ndepth
    nb = centers.shape[0]
    unit = max(PACK, rows_out)
    units, per_unit, owners = xdev // unit, unit // PACK, unit // rows_out
    blocks = units * per_unit
    span = zdev // PIECES

    def at_turn(turn):
        if owners > 1:
            return turn
        return jnp.where(turn < me, turn, ndepth - 1 - turn + me)

    def rows_of(place):
        return pl.ds(pl.multiple_of(place * unit, PACK), unit)

    def piece_load(piece):
        part = pl.ds(piece * span, span)
        return pltpu.make_async_copy(field.at[part], fb.at[part], piece_sem.at[piece])

    for piece in range(PIECES):
        piece_load(piece).start()
    pairs = ((order_in, order), (live_in, live), (centers_in, centers),
             (widths_in, widths), (heights_in, heights), (colours_in, colours))
    loads = [pltpu.make_async_copy(src, dst, load_sem.at[at]) for at, (src, dst) in enumerate(pairs)]
    for load in loads:
        load.start()

    barrier = pltpu.get_barrier_semaphore()
    for step in range(1, ndepth):
        pl.semaphore_signal(barrier, inc=1, device_id={"depth": lax.rem(me + step, ndepth)}, device_id_type=MESH)
    for axis, pos, count in (("imx", mx, nimx), ("imy", my, nimy)):
        @pl.when(pos > 0)
        def _():
            pl.semaphore_signal(barrier, inc=1, device_id={axis: pos - 1}, device_id_type=MESH)

        @pl.when(pos < count - 1)
        def _():
            pl.semaphore_signal(barrier, inc=1, device_id={axis: pos + 1}, device_id_type=MESH)

    for pos, count, low, high in ((me, ndepth, zlo, zhi), (mx, nimx, flo, fhi), (my, nimy, xlo, xhi)):
        @pl.when(pos == 0)
        def _():
            low[...] = jnp.zeros(low.shape, BF16)

        @pl.when(pos == count - 1)
        def _():
            high[...] = jnp.zeros(high.shape, BF16)

    def links(axis, pos, count, down_src, up_src, low, high, at):
        to_low = pltpu.make_async_remote_copy(
            src_ref=down_src, dst_ref=high, send_sem=halo_send.at[at], recv_sem=halo_recv.at[at],
            device_id={axis: lax.rem(pos + count - 1, count)}, device_id_type=MESH)
        to_high = pltpu.make_async_remote_copy(
            src_ref=up_src, dst_ref=low, send_sem=halo_send.at[at + 1], recv_sem=halo_recv.at[at + 1],
            device_id={axis: lax.rem(pos + 1, count)}, device_id_type=MESH)
        return pos, count, to_low, to_high

    def start(link):
        pos, count, to_low, to_high = link

        @pl.when(pos > 0)
        def _():
            to_low.start()

        @pl.when(pos < count - 1)
        def _():
            to_high.start()

    def finish(link):
        pos, count, to_low, to_high = link

        @pl.when(pos > 0)
        def _():
            to_low.wait_send()
            to_high.wait_recv()

        @pl.when(pos < count - 1)
        def _():
            to_high.wait_send()
            to_low.wait_recv()

    def zlink():
        return links("depth", me, ndepth, field.at[0], field.at[zdev - 1], zlo, zhi, 0)

    def ylink():
        return links("imx", mx, nimx, face, face, flo, fhi, 2)

    def xlink():
        return links("imy", my, nimy, field.at[:, pl.ds(0, PACK)], field.at[:, pl.ds(xdev - PACK, PACK)], xlo, xhi, 4)

    for load in loads:
        load.wait()
    back = expand(order[...], xdev, ydev)
    factor = (2.0 * back - 1.0) * expand(live[0], xdev, ydev) * (step_len * LOG2E)
    flag[...] = back
    scales[...] = factor
    cen = [centers[j] for j in range(nb)]
    hei = [heights[j] for j in range(nb)]
    cur = []
    for j in range(nb):
        wid = jnp.full((PACK, ydev), widths[j], F32)
        cur.append((-0.5 * LOG2E) / (wid * wid))
    lane = iota((PACK, ydev), 1)

    def absorb(row):
        here = pl.ds(pl.multiple_of(row, PACK), PACK)
        body = pl.ds(pl.multiple_of(row + SUB, SUB), PACK)
        fac = scales[here]
        amount = [hei[j] * fac for j in range(nb)]

        def sample(z, carry):
            depth, gone = carry
            val = fb[z, here].astype(F32)
            vf[z + 1, body] = val
            terms = []
            for j in range(nb):
                off = val - cen[j]
                if j == 0:
                    slopes[z, here] = pltpu.roll(off, ydev - 1, 1) - pltpu.roll(off, 1, 1)
                bump = jnp.exp2(off * cur[j] * off)
                lobes[j, z, here] = bump
                terms.append(amount[j] * bump)
            while len(terms) > 1:
                terms = [sum(terms[at:at + 2][1:], terms[at]) for at in range(0, len(terms), 2)]
            depth = depth + terms[0]
            now = jnp.exp2(depth)
            weights[z, here] = now - gone
            return depth, now

        zero = jnp.zeros((PACK, ydev), F32)
        depth, _ = lax.fori_loop(0, zdev, sample, (zero, zero + 1.0), unroll=UNROLL_A)
        mark = flag[here] > 0.5
        scales[here] = jnp.where(mark, jnp.exp2(-depth), -1.0)
        logs[here] = jnp.where(mark, -depth, depth) * (1.0 / LOG2E)

    def log_copy(owner, source):
        return pltpu.make_async_remote_copy(
            src_ref=logs.at[pl.ds(pl.multiple_of(owner * rows_out, SUB), rows_out)], dst_ref=logs_in.at[source],
            send_sem=log_send.at[owner], recv_sem=log_recv.at[source], device_id={"depth": owner}, device_id_type=MESH)

    def send_logs(turn, carry):
        for sub in range(owners):
            owner = at_turn(turn) * owners + sub

            @pl.when(owner != me)
            def _():
                log_copy(owner, me).start()

        return carry

    def absorb_turn(turn, carry):
        place = at_turn(turn)

        def one(i, inside):
            absorb(place * unit + i * PACK)
            return inside

        return lax.fori_loop(0, per_unit, one, carry)

    wide = iota((xdev, ydev), 1) // 2
    packed = jnp.zeros((xdev, ydev), BF16)
    for piece in range(PIECES):
        piece_load(piece).wait()
        for z in range(piece * span, piece * span + span):
            packed = jnp.where(wide == z, pltpu.roll(fb[z], 2 * z + 1, 1), packed)
    face[...] = packed

    peers = ndepth - 1
    for pos, count in ((mx, nimx), (my, nimy)):
        peers = peers + (pos + count - 1) // count + (2 * count - 2 - pos) // count
    pl.semaphore_wait(barrier, peers)
    start(ylink())
    start(zlink())
    start(xlink())

    def next_turn(turn, carry):
        absorb_turn(turn, carry)
        return send_logs(turn, carry)

    lax.fori_loop(0, units, next_turn, 0)

    outermost = (lane == 0) | (lane == ydev - 1)

    def row_of(at):
        return at_turn(at // per_unit) * unit + at % per_unit * PACK

    def patch(first, count, row):
        here = pl.ds(pl.multiple_of(row, PACK), PACK)
        outer = edges[here]
        for z in range(count):
            edge = pltpu.roll(outer, ydev - 1 - 2 * (first + z), 1)
            pltpu.store(slopes.at[first + z, here], slopes[first + z, here] + edge, mask=outermost)

    def block(at):
        row = row_of(at)
        following = row_of(jnp.minimum(at + 1, blocks - 1))
        here = pl.ds(pl.multiple_of(row, PACK), PACK)
        body = pl.ds(pl.multiple_of(row + SUB, SUB), PACK)
        above = pl.ds(row + SUB - 1, PACK)
        below = pl.ds(row + SUB + 1, PACK)

        def chunk(c, carry):
            prev, val, sums = carry
            for i in range(CHUNK):
                z = c * CHUNK + i
                after = vf[z + 2, body]
                dz = after - prev
                dx = vf[z + 1, below] - vf[z + 1, above]
                dy = slopes[z, here]
                facing = (0.7 * 0.64) * dz + (0.7 * 0.48) * dx + (0.7 * 0.6) * dy
                shade = 0.3 + jnp.abs(facing) * lax.rsqrt(dz * dz + dx * dx + dy * dy + 4.0)
                weight = weights[z, here] * shade.astype(BF16).astype(F32)
                sums = tuple(acc + weight * lobes[j, z, here] for j, acc in enumerate(sums))
                prev, val = val, after
            patch(c * CHUNK, CHUNK, following)
            return prev, val, sums

        zero = jnp.zeros((PACK, ydev), F32)
        init = (vf[0, body], vf[1, body], (zero,) * nb)
        _, _, sums = lax.fori_loop(0, zdev // CHUNK, chunk, init)
        scale = scales[here]
        spot = pl.ds(pl.multiple_of(at % per_unit * PACK, PACK), PACK)
        for chan in range(3):
            total = None
            for j in range(nb):
                term = colours[j, chan] * sums[j]
                total = term if total is None else total + term
            stage[chan, spot] = total * scale

    def sends(owner, source):
        place = {"depth": owner}
        return (
            pltpu.make_async_remote_copy(
                src_ref=tiles_out.at[owner], dst_ref=tiles_in.at[source], send_sem=tile_send.at[owner],
                recv_sem=tile_recv.at[source], device_id=place, device_id_type=MESH),
            pltpu.make_async_remote_copy(
                src_ref=peaks_out.at[owner], dst_ref=peaks_in.at[source], send_sem=peak_send.at[owner],
                recv_sem=peak_recv.at[source], device_id=place, device_id_type=MESH),
        )

    tiles_in[me] = jnp.zeros((3, rows_out, ydev), jnp.int16)
    peaks_in[me] = jnp.zeros((SUB, ydev), F32)
    finish(xlink())

    def widen_rows(z, carry):
        vf[z + 1, 0:SUB] = xlo[z].astype(F32)[PACK - SUB:]
        vf[z + 1, SUB + xdev:] = xhi[z].astype(F32)[:SUB]
        return carry

    lax.fori_loop(0, zdev, widen_rows, 0, unroll=8)
    finish(zlink())
    vf[0, SUB:SUB + xdev] = zlo[...].astype(F32)
    vf[zdev + 1, SUB:SUB + xdev] = zhi[...].astype(F32)
    finish(ylink())
    mine = face[...].astype(F32)
    low = pltpu.roll(mine - flo[...].astype(F32), 1, 1)
    high = pltpu.roll(fhi[...].astype(F32) - mine, ydev - 1, 1)
    edges[...] = jnp.where(iota((xdev, ydev), 1) % 2 == 0, high, low)
    patch(0, zdev, row_of(0))

    def tile_turn(turn):
        place = at_turn(turn)
        for sub in range(owners):
            owner = place * owners + sub
            part = pl.ds(sub * rows_out, rows_out)

            @pl.when(owner == me)
            def _():
                own[...] = stage[:, part]

            @pl.when(owner != me)
            def _():
                line = iota((SUB, ydev), 0)
                peaks = jnp.zeros((SUB, ydev), F32)
                for chan in range(3):
                    value = stage[chan, part]
                    peak = jnp.maximum(jnp.max(value, axis=0, keepdims=True), 1e-30)
                    peaks = jnp.where(line == chan, peak * (1.0 / LEVELS), peaks)
                    tiles_out[owner, chan] = (value * (LEVELS / peak) + 0.5).astype(jnp.int32).astype(jnp.int16)
                peaks_out[owner] = peaks
                for copy in sends(owner, me):
                    copy.start()

    def step(at, carry):
        turn = at // per_unit
        final = at % per_unit == per_unit - 1

        block(at)

        @pl.when(final)
        def _():
            tile_turn(turn)

        return carry

    lax.fori_loop(0, blocks, step, 0)

    for step_on in range(1, ndepth):
        owner = lax.rem(me + step_on, ndepth)
        for copy in sends(owner, owner):
            copy.wait()
        log_copy(owner, owner).wait()

    logs_in[me] = logs[pl.ds(pl.multiple_of(me * rows_out, SUB), rows_out)]
    mark = flag[pl.ds(pl.multiple_of(me * rows_out, SUB), rows_out)] > 0.5
    zero = jnp.zeros((rows_out, ydev), F32)
    done, through, total = [zero] * 3, zero + 1.0, zero
    for slab in range(ndepth):
        logt = logs_in[slab]
        clear = jnp.exp(logt)
        keep = jnp.where(mark, clear, 1.0)
        ahead = jnp.where(mark, 1.0, through)
        for chan in range(3):
            value = tiles_in[slab, chan].astype(jnp.int32).astype(F32) * peaks_in[slab, chan:chan + 1]
            value = jnp.where(me == slab, own[chan], value)
            done[chan] = keep * done[chan] + ahead * value
        through = through * clear
        total = total + logt
    for chan in range(3):
        colour_out[chan] = done[chan]
    logt_out[...] = total


def local(field, brick_live, order, centers, widths, heights, colours):
    counts = tuple(lax.axis_size(axis) for axis in ("depth", "imx", "imy"))
    zdev, xdev, ydev = field.shape
    ndepth = counts[0]
    rows_out = xdev // ndepth
    step_len = OPTICAL / (zdev * ndepth)
    unit = max(PACK, rows_out)
    units = xdev // unit
    vmem = pl.BlockSpec(memory_space=pltpu.VMEM)
    dma = pltpu.SemaphoreType.DMA
    return pl.pallas_call(
        functools.partial(kernel, counts, step_len),
        out_shape=(
            pltpu.VMEM((3, rows_out, ydev), F32),
            pltpu.VMEM((rows_out, ydev), F32),
        ),
        in_specs=[pl.BlockSpec(memory_space=pl.ANY)] * 7,
        out_specs=(vmem, vmem),
        scratch_shapes=[
            pltpu.VMEM((zdev, xdev, ydev), BF16),
            pltpu.VMEM(brick_live.shape, jnp.int32),
            pltpu.VMEM(order.shape, jnp.int32),
            pltpu.SMEM(centers.shape, F32),
            pltpu.SMEM(widths.shape, F32),
            pltpu.SMEM(heights.shape, F32),
            pltpu.SMEM(colours.shape, F32),
            pltpu.VMEM((zdev + 2, xdev + 2 * SUB, ydev), F32),
            pltpu.VMEM((xdev, ydev), BF16),
            pltpu.VMEM((xdev, ydev), BF16),
            pltpu.VMEM((zdev, PACK, ydev), BF16),
            pltpu.VMEM((zdev, PACK, ydev), BF16),
            pltpu.VMEM((xdev, ydev), BF16),
            pltpu.VMEM((xdev, ydev), BF16),
            pltpu.VMEM((xdev, ydev), BF16),
            pltpu.VMEM((xdev, ydev), F32),
            pltpu.VMEM((zdev, xdev, ydev), F32),
            pltpu.VMEM((zdev, xdev, ydev), F32),
            pltpu.VMEM((centers.shape[0], zdev, xdev, ydev), F32),
            pltpu.VMEM((xdev, ydev), F32),
            pltpu.VMEM((xdev, ydev), F32),
            pltpu.VMEM((xdev, ydev), F32),
            pltpu.VMEM((ndepth, rows_out, ydev), F32),
            pltpu.VMEM((ndepth, 3, rows_out, ydev), jnp.int16),
            pltpu.VMEM((ndepth, 3, rows_out, ydev), jnp.int16),
            pltpu.VMEM((3, unit, ydev), F32),
            pltpu.VMEM((3, rows_out, ydev), F32),
            pltpu.VMEM((ndepth, SUB, ydev), F32),
            pltpu.VMEM((ndepth, SUB, ydev), F32),
            dma((6,)),
            dma((PIECES,)),
            dma((6,)),
            dma((6,)),
            dma((ndepth,)),
            dma((ndepth,)),
            dma((ndepth,)),
            dma((ndepth,)),
            dma((ndepth,)),
            dma((ndepth,)),
        ],
        compiler_params=pltpu.CompilerParams(collective_id=0, has_side_effects=True),
    )(field, brick_live, order, centers, widths, heights, colours)


def solution(mesh):
    return jax.shard_map(
        local,
        mesh=mesh,
        in_specs=(
            P("depth", "imy", "imx"),
            P("depth", "imy", "imx"),
            P("imy", "imx"),
            P(),
            P(),
            P(),
            P(),
        ),
        out_specs=(P(None, ("imy", "depth"), "imx"), P(("imy", "depth"), "imx")),
        check_vma=False,
    )
```

```python
import functools
import math

import jax
import jax.numpy as jnp
from jax import lax
from jax.experimental import pallas as pl
from jax.experimental.pallas import tpu as pltpu
from jax.sharding import PartitionSpec as P

OPTICAL = 3.0
MESH = pl.DeviceIdType.MESH
SUB = 8
PACK = 16
F32 = jnp.float32
BF16 = jnp.bfloat16
LEVELS = 32000.0
UNROLL_A = 16
CHUNK = 16
PIECES = 4
EARLY = 0
LOG2E = math.log2(math.e)


def iota(shape, dim):
    return lax.broadcasted_iota(jnp.int32, shape, dim)


def expand(small, rows, cols):
    high, wide = small.shape
    down = (iota((rows, high), 0) // (rows // high) == iota((rows, high), 1)).astype(F32).astype(BF16)
    along = (iota((wide, cols), 1) // (cols // wide) == iota((wide, cols), 0)).astype(F32).astype(BF16)
    tall = jnp.dot(down, small.astype(F32).astype(BF16), preferred_element_type=F32)
    return jnp.dot(tall.astype(BF16), along, preferred_element_type=F32)


def kernel(
    counts, step_len,
    field, live_in, order_in, centers_in, widths_in, heights_in, colours_in,
    colour_out, logt_out,
    fb, live, order, centers, widths, heights, colours,
    vf, zlo, zhi, xlo, xhi, face, flo, fhi, edges, slopes, splats, weights, lobes, scales, flag, logs, logs_in,
    tiles_out, tiles_in, stage, own,
    load_sem, piece_sem, halo_send, halo_recv, log_send, log_recv, tile_send, tile_recv,
):
    ndepth, nimx, nimy = counts
    me = lax.axis_index("depth")
    mx = lax.axis_index("imx")
    my = lax.axis_index("imy")
    zdev, xdev, ydev = fb.shape
    rows_out = xdev // ndepth
    nb = centers.shape[0]
    unit = max(PACK, rows_out)
    units, per_unit, owners = xdev // unit, unit // PACK, unit // rows_out
    blocks = units * per_unit
    span = zdev // PIECES
    early = jnp.clip(ndepth - 1 - 2 * me, 0, min(EARLY, units))
    plane = max(PACK, rows_out)

    def at_turn(turn):
        if owners > 1:
            return turn
        return jnp.where(turn < me, turn, ndepth - 1 - turn + me)

    def rows_of(place):
        return pl.ds(pl.multiple_of(place * unit, PACK), unit)

    def piece_load(piece):
        part = pl.ds(piece * span, span)
        return pltpu.make_async_copy(field.at[part], fb.at[part], piece_sem.at[piece])

    barrier = pltpu.get_barrier_semaphore()
    for axis, pos, count in (("imx", mx, nimx), ("imy", my, nimy)):
        @pl.when(pos > 0)
        def _():
            pl.semaphore_signal(barrier, inc=1, device_id={axis: pos - 1}, device_id_type=MESH)

        @pl.when(pos < count - 1)
        def _():
            pl.semaphore_signal(barrier, inc=1, device_id={axis: pos + 1}, device_id_type=MESH)

    for step in range(1, ndepth):
        pl.semaphore_signal(barrier, inc=1, device_id={"depth": lax.rem(me + step, ndepth)}, device_id_type=MESH)

    pairs = ((order_in, order), (live_in, live), (centers_in, centers),
             (widths_in, widths), (heights_in, heights), (colours_in, colours))
    loads = [pltpu.make_async_copy(src, dst, load_sem.at[at]) for at, (src, dst) in enumerate(pairs)]
    for load in loads:
        load.start()
    for piece in range(PIECES):
        piece_load(piece).start()

    for pos, count, low, high in ((me, ndepth, zlo, zhi), (mx, nimx, flo, fhi), (my, nimy, xlo, xhi)):
        @pl.when(pos == 0)
        def _():
            low[...] = jnp.zeros(low.shape, BF16)

        @pl.when(pos == count - 1)
        def _():
            high[...] = jnp.zeros(high.shape, BF16)

    def links(axis, pos, count, down_src, up_src, low, high, at):
        to_low = pltpu.make_async_remote_copy(
            src_ref=down_src, dst_ref=high, send_sem=halo_send.at[at], recv_sem=halo_recv.at[at],
            device_id={axis: lax.rem(pos + count - 1, count)}, device_id_type=MESH)
        to_high = pltpu.make_async_remote_copy(
            src_ref=up_src, dst_ref=low, send_sem=halo_send.at[at + 1], recv_sem=halo_recv.at[at + 1],
            device_id={axis: lax.rem(pos + 1, count)}, device_id_type=MESH)
        return pos, count, to_low, to_high

    def start(link):
        pos, count, to_low, to_high = link

        @pl.when(pos > 0)
        def _():
            to_low.start()

        @pl.when(pos < count - 1)
        def _():
            to_high.start()

    def finish(link):
        pos, count, to_low, to_high = link

        @pl.when(pos > 0)
        def _():
            to_low.wait_send()
            to_high.wait_recv()

        @pl.when(pos < count - 1)
        def _():
            to_high.wait_send()
            to_low.wait_recv()

    def zlink(place):
        rows = rows_of(place)
        return links("depth", me, ndepth, field.at[0, rows], field.at[zdev - 1, rows], zlo.at[rows], zhi.at[rows], 2 * place)

    def ylink(place):
        rows = rows_of(place)
        return links("imx", mx, nimx, face.at[rows], face.at[rows], flo.at[rows], fhi.at[rows], 2 * units + 2 * place)

    def xlink():
        return links("imy", my, nimy, field.at[:, pl.ds(0, PACK)], field.at[:, pl.ds(xdev - PACK, PACK)], xlo, xhi, 4 * units)

    for load in loads:
        load.wait()
    back = expand(order[...], xdev, ydev)
    factor = (2.0 * back - 1.0) * expand(live[0], xdev, ydev) * (step_len * LOG2E)
    flag[...] = back
    scales[...] = factor
    for j in range(nb):
        wid = jnp.full((PACK, ydev), widths[j], F32)
        splats[0, j] = jnp.full((PACK, ydev), centers[j], F32)
        splats[1, j] = (-0.5 * LOG2E) / (wid * wid)
    lane = iota((PACK, ydev), 1)

    def absorb(row):
        here = pl.ds(pl.multiple_of(row, PACK), PACK)
        body = pl.ds(pl.multiple_of(row + SUB, SUB), PACK)
        fac = scales[here]
        for j in range(nb):
            splats[2, j] = heights[j] * fac

        def sample(z, carry):
            depth, gone = carry
            val = fb[z, here].astype(F32)
            vf[z + 1, body] = val
            terms = []
            for j in range(nb):
                off = val - splats[0, j]
                if j == 0:
                    slopes[z, here] = pltpu.roll(off, ydev - 1, 1) - pltpu.roll(off, 1, 1)
                bump = jnp.exp2(off * splats[1, j] * off)
                lobes[j, z, here] = bump
                terms.append(splats[2, j] * bump)
            while len(terms) > 1:
                terms = [sum(terms[at:at + 2][1:], terms[at]) for at in range(0, len(terms), 2)]
            depth = depth + terms[0]
            now = jnp.exp2(depth)
            weights[z, here] = now - gone
            return depth, now

        zero = jnp.zeros((PACK, ydev), F32)
        depth, _ = lax.fori_loop(0, zdev, sample, (zero, zero + 1.0), unroll=UNROLL_A)
        mark = flag[here] > 0.5
        scales[here] = jnp.where(mark, jnp.exp2(-depth), -1.0)
        logs[here] = jnp.where(mark, -depth, depth) * (1.0 / LOG2E)

    def log_copy(owner, source):
        return pltpu.make_async_remote_copy(
            src_ref=logs.at[pl.ds(pl.multiple_of(owner * rows_out, SUB), rows_out)], dst_ref=logs_in.at[source],
            send_sem=log_send.at[owner], recv_sem=log_recv.at[source], device_id={"depth": owner}, device_id_type=MESH)

    def send_logs(turn, carry):
        for sub in range(owners):
            owner = at_turn(turn) * owners + sub

            @pl.when(owner != me)
            def _():
                log_copy(owner, me).start()

        return carry

    def absorb_turn(turn, carry):
        place = at_turn(turn)

        def one(i, inside):
            absorb(place * unit + i * PACK)
            return inside

        return lax.fori_loop(0, per_unit, one, carry)

    wide = iota((xdev, ydev), 1) // 2
    packed = jnp.zeros((xdev, ydev), BF16)
    for piece in range(PIECES):
        piece_load(piece).wait()
        for z in range(piece * span, piece * span + span):
            packed = jnp.where(wide == z, pltpu.roll(fb[z], 2 * z + 1, 1), packed)
    face[...] = packed

    if EARLY:
        lax.fori_loop(0, early, absorb_turn, 0)
    peers = ndepth - 1
    for pos, count in ((mx, nimx), (my, nimy)):
        peers = peers + (pos + count - 1) // count + (2 * count - 2 - pos) // count
    pl.semaphore_wait(barrier, peers)

    def start_turn(turn, carry):
        start(ylink(at_turn(turn)))
        start(zlink(at_turn(turn)))
        return carry

    start_turn(0, 0)
    start(xlink())
    lax.fori_loop(1, units, start_turn, 0)
    if EARLY:
        lax.fori_loop(0, early, send_logs, 0)

    def next_turn(turn, carry):
        absorb_turn(turn, carry)
        return send_logs(turn, carry)

    lax.fori_loop(early if EARLY else 0, units, next_turn, 0)

    outermost = (lane == 0) | (lane == ydev - 1)

    def row_of(at):
        return at_turn(at // per_unit) * unit + at % per_unit * PACK

    def patch(first, count, row):
        here = pl.ds(pl.multiple_of(row, PACK), PACK)
        outer = edges[here]
        for z in range(count):
            edge = pltpu.roll(outer, ydev - 1 - 2 * (first + z), 1)
            pltpu.store(slopes.at[first + z, here], slopes[first + z, here] + edge, mask=outermost)

    def block(at):
        row = row_of(at)
        following = row_of(jnp.minimum(at + 1, blocks - 1))
        here = pl.ds(pl.multiple_of(row, PACK), PACK)
        body = pl.ds(pl.multiple_of(row + SUB, SUB), PACK)
        above = pl.ds(row + SUB - 1, PACK)
        below = pl.ds(row + SUB + 1, PACK)

        def chunk(c, carry):
            prev, val, sums = carry
            for i in range(CHUNK):
                z = c * CHUNK + i
                after = vf[z + 2, body]
                dz = after - prev
                dx = vf[z + 1, below] - vf[z + 1, above]
                dy = slopes[z, here]
                facing = (0.7 * 0.64) * dz + (0.7 * 0.48) * dx + (0.7 * 0.6) * dy
                shade = 0.3 + jnp.abs(facing) * lax.rsqrt(dz * dz + dx * dx + dy * dy + 4.0)
                weight = weights[z, here] * shade.astype(BF16).astype(F32)
                sums = tuple(acc + weight * lobes[j, z, here] for j, acc in enumerate(sums))
                prev, val = val, after
            patch(c * CHUNK, CHUNK, following)
            return prev, val, sums

        zero = jnp.zeros((PACK, ydev), F32)
        init = (vf[0, body], vf[1, body], (zero,) * nb)
        _, _, sums = lax.fori_loop(0, zdev // CHUNK, chunk, init)
        scale = scales[here]
        spot = pl.ds(pl.multiple_of(at % per_unit * PACK, PACK), PACK)
        for chan in range(3):
            total = None
            for j in range(nb):
                term = colours[j, chan] * sums[j]
                total = term if total is None else total + term
            stage[chan, spot] = total * scale

    def tile_copy(owner, source):
        return pltpu.make_async_remote_copy(
            src_ref=tiles_out.at[owner], dst_ref=tiles_in.at[source], send_sem=tile_send.at[owner],
            recv_sem=tile_recv.at[source], device_id={"depth": owner}, device_id_type=MESH)

    tiles_in[me] = jnp.zeros(tiles_in.shape[1:], jnp.int16)
    finish(xlink())

    def widen_rows(z, carry):
        vf[z + 1, 0:SUB] = xlo[z].astype(F32)[PACK - SUB:]
        vf[z + 1, SUB + xdev:] = xhi[z].astype(F32)[:SUB]
        return carry

    lax.fori_loop(0, zdev, widen_rows, 0, unroll=8)
    def ready(turn):
        place = at_turn(turn)
        rows = rows_of(place)
        body = pl.ds(pl.multiple_of(place * unit + SUB, SUB), unit)
        finish(zlink(place))
        vf[0, body] = zlo[rows].astype(F32)
        vf[zdev + 1, body] = zhi[rows].astype(F32)
        finish(ylink(place))
        mine = face[rows].astype(F32)
        low = pltpu.roll(mine - flo[rows].astype(F32), 1, 1)
        high = pltpu.roll(fhi[rows].astype(F32) - mine, ydev - 1, 1)
        edges[rows] = jnp.where(iota((unit, ydev), 1) % 2 == 0, high, low)

    ready(0)
    patch(0, zdev, row_of(0))

    def tile_turn(turn):
        place = at_turn(turn)
        for sub in range(owners):
            owner = place * owners + sub
            part = pl.ds(sub * rows_out, rows_out)

            @pl.when(owner == me)
            def _():
                own[...] = stage[:, part]

            @pl.when(owner != me)
            def _():
                line = iota((PACK, ydev), 0)
                powers = jnp.zeros((PACK, ydev), F32)
                for chan in range(3):
                    value = stage[chan, part]
                    peak = jnp.maximum(jnp.max(value, axis=0, keepdims=True), 1e-30)
                    power = jnp.ceil(jnp.log2(peak * (1.0 / LEVELS)))
                    powers = jnp.where(line == chan, power, powers)
                    level = (value * jnp.exp2(-power) + 0.5).astype(jnp.int32)
                    tiles_out[owner, chan * plane:chan * plane + rows_out] = level.astype(jnp.int16)
                tiles_out[owner, 3 * plane:] = powers.astype(jnp.int32).astype(jnp.int16)
                tile_copy(owner, me).start()

    def step(at, carry):
        turn = at // per_unit
        final = at % per_unit == per_unit - 1

        @pl.when(final & (turn < units - 1))
        def _():
            ready(turn + 1)

        block(at)

        @pl.when(final)
        def _():
            tile_turn(turn)

        return carry

    lax.fori_loop(0, blocks, step, 0)

    logs_in[me] = logs[pl.ds(pl.multiple_of(me * rows_out, SUB), rows_out)]
    mark = flag[pl.ds(pl.multiple_of(me * rows_out, SUB), rows_out)] > 0.5
    zero = jnp.zeros((rows_out, ydev), F32)
    done, through, total = [zero] * 3, zero + 1.0, zero
    for slab in range(ndepth):
        @pl.when(me != slab)
        def _():
            log_copy(slab, slab).wait()
            tile_copy(slab, slab).wait()

        logt = logs_in[slab]
        clear = jnp.exp(logt)
        keep = jnp.where(mark, clear, 1.0)
        ahead = jnp.where(mark, 1.0, through)
        powers = jnp.exp2(tiles_in[slab, 3 * plane:].astype(jnp.int32).astype(F32))
        for chan in range(3):
            level = tiles_in[slab, chan * plane:chan * plane + rows_out].astype(jnp.int32).astype(F32)
            value = jnp.where(me == slab, own[chan], level * powers[chan:chan + 1])
            done[chan] = keep * done[chan] + ahead * value
        through = through * clear
        total = total + logt
    for chan in range(3):
        colour_out[chan] = done[chan]
    logt_out[...] = total


def hand_over(colour, logt, colour_out, logt_out, sem):
    copies = [pltpu.make_async_copy(src, dst, sem.at[at])
              for at, (src, dst) in enumerate(((colour, colour_out), (logt, logt_out)))]
    for copy in copies:
        copy.start()
    for copy in copies:
        copy.wait()


def local(field, brick_live, order, centers, widths, heights, colours):
    counts = tuple(lax.axis_size(axis) for axis in ("depth", "imx", "imy"))
    zdev, xdev, ydev = field.shape
    ndepth = counts[0]
    rows_out = xdev // ndepth
    step_len = OPTICAL / (zdev * ndepth)
    unit = max(PACK, rows_out)
    units = xdev // unit
    vmem = pl.BlockSpec(memory_space=pltpu.VMEM)
    dma = pltpu.SemaphoreType.DMA
    done = pl.pallas_call(
        functools.partial(kernel, counts, step_len),
        out_shape=(
            pltpu.VMEM((3, rows_out, ydev), F32),
            pltpu.VMEM((rows_out, ydev), F32),
        ),
        in_specs=[pl.BlockSpec(memory_space=pl.ANY)] * 7,
        out_specs=(vmem, vmem),
        scratch_shapes=[
            pltpu.VMEM((zdev, xdev, ydev), BF16),
            pltpu.VMEM(brick_live.shape, jnp.int32),
            pltpu.VMEM(order.shape, jnp.int32),
            pltpu.SMEM(centers.shape, F32),
            pltpu.SMEM(widths.shape, F32),
            pltpu.SMEM(heights.shape, F32),
            pltpu.SMEM(colours.shape, F32),
            pltpu.VMEM((zdev + 2, xdev + 2 * SUB, ydev), F32),
            pltpu.VMEM((xdev, ydev), BF16),
            pltpu.VMEM((xdev, ydev), BF16),
            pltpu.VMEM((zdev, PACK, ydev), BF16),
            pltpu.VMEM((zdev, PACK, ydev), BF16),
            pltpu.VMEM((xdev, ydev), BF16),
            pltpu.VMEM((xdev, ydev), BF16),
            pltpu.VMEM((xdev, ydev), BF16),
            pltpu.VMEM((xdev, ydev), F32),
            pltpu.VMEM((zdev, xdev, ydev), F32),
            pltpu.VMEM((3, centers.shape[0], PACK, ydev), F32),
            pltpu.VMEM((zdev, xdev, ydev), F32),
            pltpu.VMEM((centers.shape[0], zdev, xdev, ydev), F32),
            pltpu.VMEM((xdev, ydev), F32),
            pltpu.VMEM((xdev, ydev), F32),
            pltpu.VMEM((xdev, ydev), F32),
            pltpu.VMEM((ndepth, rows_out, ydev), F32),
            pltpu.VMEM((ndepth, 3 * max(PACK, rows_out) + PACK, ydev), jnp.int16),
            pltpu.VMEM((ndepth, 3 * max(PACK, rows_out) + PACK, ydev), jnp.int16),
            pltpu.VMEM((3, unit, ydev), F32),
            pltpu.VMEM((3, rows_out, ydev), F32),
            dma((6,)),
            dma((PIECES,)),
            dma((4 * units + 2,)),
            dma((4 * units + 2,)),
            dma((ndepth,)),
            dma((ndepth,)),
            dma((ndepth,)),
            dma((ndepth,)),
        ],
        compiler_params=pltpu.CompilerParams(collective_id=0, has_side_effects=True),
    )(field, brick_live, order, centers, widths, heights, colours)
    return pl.pallas_call(
        hand_over,
        out_shape=tuple(jax.ShapeDtypeStruct(part.shape, F32) for part in done),
        in_specs=[vmem] * 2,
        out_specs=(pl.BlockSpec(memory_space=pl.ANY),) * 2,
        scratch_shapes=[dma((2,))],
    )(*(pltpu.with_memory_space_constraint(part, pltpu.VMEM) for part in done))


def solution(mesh):
    return jax.shard_map(
        local,
        mesh=mesh,
        in_specs=(
            P("depth", "imy", "imx"),
            P("depth", "imy", "imx"),
            P("imy", "imx"),
            P(),
            P(),
            P(),
            P(),
        ),
        out_specs=(P(None, ("imy", "depth"), "imx"), P(("imy", "depth"), "imx")),
        check_vma=False,
    )
```

```python
import functools
import math

import jax
import jax.numpy as jnp
from jax import lax
from jax.experimental import pallas as pl
from jax.experimental.pallas import tpu as pltpu
from jax.sharding import PartitionSpec as P

OPTICAL = 3.0
MESH = pl.DeviceIdType.MESH
SUB = 8
PACK = 16
F32 = jnp.float32
BF16 = jnp.bfloat16
LEVELS = 32000.0
UNROLL_A = 16
CHUNK = 16
PIECES = 2
EARLY = 0
LOG2E = math.log2(math.e)


def iota(shape, dim):
    return lax.broadcasted_iota(jnp.int32, shape, dim)


def expand(small, rows, cols):
    high, wide = small.shape
    down = (iota((rows, high), 0) // (rows // high) == iota((rows, high), 1)).astype(F32).astype(BF16)
    along = (iota((wide, cols), 1) // (cols // wide) == iota((wide, cols), 0)).astype(F32).astype(BF16)
    tall = jnp.dot(down, small.astype(F32).astype(BF16), preferred_element_type=F32)
    return jnp.dot(tall.astype(BF16), along, preferred_element_type=F32)


def kernel(
    counts, step_len,
    field, live_in, order_in, centers_in, widths_in, heights_in, colours_in,
    colour_out, logt_out,
    fb, live, order, centers, widths, heights, colours,
    vf, zlo, zhi, xlo, xhi, face, flo, fhi, edges, slopes, splats, weights, lobes, scales, flag, logs, logs_in,
    tiles_out, tiles_in, stage, own,
    load_sem, piece_sem, halo_send, halo_recv, log_send, log_recv, tile_send, tile_recv,
):
    ndepth, nimx, nimy = counts
    me = lax.axis_index("depth")
    mx = lax.axis_index("imx")
    my = lax.axis_index("imy")
    zdev, xdev, ydev = fb.shape
    rows_out = xdev // ndepth
    nb = centers.shape[0]
    unit = max(PACK, rows_out)
    units, per_unit, owners = xdev // unit, unit // PACK, unit // rows_out
    blocks = units * per_unit
    span = zdev // PIECES
    early = jnp.clip(ndepth - 1 - 2 * me, 0, min(EARLY, units))
    plane = max(PACK, rows_out)

    def at_turn(turn):
        if owners > 1:
            return turn
        return jnp.where(turn < me, turn, ndepth - 1 - turn + me)

    def rows_of(place):
        return pl.ds(pl.multiple_of(place * unit, PACK), unit)

    def piece_load(piece):
        part = pl.ds(piece * span, span)
        return pltpu.make_async_copy(field.at[part], fb.at[part], piece_sem.at[piece])

    barrier = pltpu.get_barrier_semaphore()
    for axis, pos, count in (("imx", mx, nimx), ("imy", my, nimy)):
        @pl.when(pos > 0)
        def _():
            pl.semaphore_signal(barrier, inc=1, device_id={axis: pos - 1}, device_id_type=MESH)

        @pl.when(pos < count - 1)
        def _():
            pl.semaphore_signal(barrier, inc=1, device_id={axis: pos + 1}, device_id_type=MESH)

    for step in range(1, ndepth):
        pl.semaphore_signal(barrier, inc=1, device_id={"depth": lax.rem(me + step, ndepth)}, device_id_type=MESH)

    pairs = ((order_in, order), (live_in, live), (centers_in, centers),
             (widths_in, widths), (heights_in, heights), (colours_in, colours))
    loads = [pltpu.make_async_copy(src, dst, load_sem.at[at]) for at, (src, dst) in enumerate(pairs)]
    for load in loads:
        load.start()
    for piece in range(PIECES):
        piece_load(piece).start()

    for pos, count, low, high in ((me, ndepth, zlo, zhi), (mx, nimx, flo, fhi), (my, nimy, xlo, xhi)):
        @pl.when(pos == 0)
        def _():
            low[...] = jnp.zeros(low.shape, BF16)

        @pl.when(pos == count - 1)
        def _():
            high[...] = jnp.zeros(high.shape, BF16)

    def links(axis, pos, count, down_src, up_src, low, high, at):
        to_low = pltpu.make_async_remote_copy(
            src_ref=down_src, dst_ref=high, send_sem=halo_send.at[at], recv_sem=halo_recv.at[at],
            device_id={axis: lax.rem(pos + count - 1, count)}, device_id_type=MESH)
        to_high = pltpu.make_async_remote_copy(
            src_ref=up_src, dst_ref=low, send_sem=halo_send.at[at + 1], recv_sem=halo_recv.at[at + 1],
            device_id={axis: lax.rem(pos + 1, count)}, device_id_type=MESH)
        return pos, count, to_low, to_high

    def start(link):
        pos, count, to_low, to_high = link

        @pl.when(pos > 0)
        def _():
            to_low.start()

        @pl.when(pos < count - 1)
        def _():
            to_high.start()

    def finish(link):
        pos, count, to_low, to_high = link

        @pl.when(pos > 0)
        def _():
            to_low.wait_send()
            to_high.wait_recv()

        @pl.when(pos < count - 1)
        def _():
            to_high.wait_send()
            to_low.wait_recv()

    def zlink(place):
        rows = rows_of(place)
        return links("depth", me, ndepth, field.at[0, rows], field.at[zdev - 1, rows], zlo.at[rows], zhi.at[rows], 2 * place)

    def ylink(place):
        rows = rows_of(place)
        return links("imx", mx, nimx, face.at[rows], face.at[rows], flo.at[rows], fhi.at[rows], 2 * units + 2 * place)

    def xlink():
        return links("imy", my, nimy, field.at[:, pl.ds(0, PACK)], field.at[:, pl.ds(xdev - PACK, PACK)], xlo, xhi, 4 * units)

    for load in loads:
        load.wait()
    back = expand(order[...], xdev, ydev)
    factor = (2.0 * back - 1.0) * expand(live[0], xdev, ydev) * (step_len * LOG2E)
    flag[...] = back
    scales[...] = factor
    for j in range(nb):
        wid = jnp.full((PACK, ydev), widths[j], F32)
        splats[0, j] = jnp.full((PACK, ydev), centers[j], F32)
        splats[1, j] = (-0.5 * LOG2E) / (wid * wid)
    lane = iota((PACK, ydev), 1)

    def absorb(row):
        here = pl.ds(pl.multiple_of(row, PACK), PACK)
        body = pl.ds(pl.multiple_of(row + SUB, SUB), PACK)
        fac = scales[here]
        for j in range(nb):
            splats[2, j] = heights[j] * fac

        def sample(z, carry):
            depth, gone = carry
            val = fb[z, here].astype(F32)
            vf[z + 1, body] = val
            terms = []
            for j in range(nb):
                off = val - splats[0, j]
                if j == 0:
                    slopes[z, here] = pltpu.roll(off, ydev - 1, 1) - pltpu.roll(off, 1, 1)
                bump = jnp.exp2(off * splats[1, j] * off)
                lobes[j, z, here] = bump
                terms.append(splats[2, j] * bump)
            while len(terms) > 1:
                terms = [sum(terms[at:at + 2][1:], terms[at]) for at in range(0, len(terms), 2)]
            depth = depth + terms[0]
            now = jnp.exp2(depth)
            weights[z, here] = now - gone
            return depth, now

        zero = jnp.zeros((PACK, ydev), F32)
        depth, _ = lax.fori_loop(0, zdev, sample, (zero, zero + 1.0), unroll=UNROLL_A)
        mark = flag[here] > 0.5
        scales[here] = jnp.where(mark, jnp.exp2(-depth), -1.0)
        logs[here] = jnp.where(mark, -depth, depth) * (1.0 / LOG2E)

    def log_copy(owner, source):
        return pltpu.make_async_remote_copy(
            src_ref=logs.at[pl.ds(pl.multiple_of(owner * rows_out, SUB), rows_out)], dst_ref=logs_in.at[source],
            send_sem=log_send.at[owner], recv_sem=log_recv.at[source], device_id={"depth": owner}, device_id_type=MESH)

    def send_logs(turn, carry):
        for sub in range(owners):
            owner = at_turn(turn) * owners + sub

            @pl.when(owner != me)
            def _():
                log_copy(owner, me).start()

        return carry

    def absorb_turn(turn, carry):
        place = at_turn(turn)

        def one(i, inside):
            absorb(place * unit + i * PACK)
            return inside

        return lax.fori_loop(0, per_unit, one, carry)

    wide = iota((xdev, ydev), 1) // 2
    packed = jnp.zeros((xdev, ydev), BF16)
    for piece in range(PIECES):
        piece_load(piece).wait()
        for z in range(piece * span, piece * span + span):
            packed = jnp.where(wide == z, pltpu.roll(fb[z], 2 * z + 1, 1), packed)
    face[...] = packed

    if EARLY:
        lax.fori_loop(0, early, absorb_turn, 0)
    peers = ndepth - 1
    for pos, count in ((mx, nimx), (my, nimy)):
        peers = peers + (pos + count - 1) // count + (2 * count - 2 - pos) // count
    pl.semaphore_wait(barrier, peers)

    def start_turn(turn, carry):
        start(zlink(at_turn(turn)))
        start(ylink(at_turn(turn)))
        return carry

    start_turn(0, 0)
    start(xlink())
    lax.fori_loop(1, units, start_turn, 0)
    if EARLY:
        lax.fori_loop(0, early, send_logs, 0)

    def next_turn(turn, carry):
        absorb_turn(turn, carry)
        return send_logs(turn, carry)

    lax.fori_loop(early if EARLY else 0, units, next_turn, 0)

    outermost = (lane == 0) | (lane == ydev - 1)

    def row_of(at):
        return at_turn(at // per_unit) * unit + at % per_unit * PACK

    def patch(first, count, row):
        here = pl.ds(pl.multiple_of(row, PACK), PACK)
        outer = edges[here]
        for z in range(count):
            edge = pltpu.roll(outer, ydev - 1 - 2 * (first + z), 1)
            pltpu.store(slopes.at[first + z, here], slopes[first + z, here] + edge, mask=outermost)

    def block(at):
        row = row_of(at)
        following = row_of(jnp.minimum(at + 1, blocks - 1))
        here = pl.ds(pl.multiple_of(row, PACK), PACK)
        body = pl.ds(pl.multiple_of(row + SUB, SUB), PACK)
        above = pl.ds(row + SUB - 1, PACK)
        below = pl.ds(row + SUB + 1, PACK)

        def chunk(c, carry):
            prev, val, sums = carry
            for i in range(CHUNK):
                z = c * CHUNK + i
                after = vf[z + 2, body]
                dz = after - prev
                dx = vf[z + 1, below] - vf[z + 1, above]
                dy = slopes[z, here]
                facing = (0.7 * 0.64) * dz + (0.7 * 0.48) * dx + (0.7 * 0.6) * dy
                shade = 0.3 + jnp.abs(facing) * lax.rsqrt(dz * dz + dx * dx + dy * dy + 4.0)
                weight = weights[z, here] * shade.astype(BF16).astype(F32)
                sums = tuple(acc + weight * lobes[j, z, here] for j, acc in enumerate(sums))
                prev, val = val, after
            patch(c * CHUNK, CHUNK, following)
            return prev, val, sums

        zero = jnp.zeros((PACK, ydev), F32)
        init = (vf[0, body], vf[1, body], (zero,) * nb)
        _, _, sums = lax.fori_loop(0, zdev // CHUNK, chunk, init)
        scale = scales[here]
        spot = pl.ds(pl.multiple_of(at % per_unit * PACK, PACK), PACK)
        for chan in range(3):
            total = None
            for j in range(nb):
                term = colours[j, chan] * sums[j]
                total = term if total is None else total + term
            stage[chan, spot] = total * scale

    def tile_copy(owner, source):
        return pltpu.make_async_remote_copy(
            src_ref=tiles_out.at[owner], dst_ref=tiles_in.at[source], send_sem=tile_send.at[owner],
            recv_sem=tile_recv.at[source], device_id={"depth": owner}, device_id_type=MESH)

    tiles_in[me] = jnp.zeros(tiles_in.shape[1:], jnp.int16)
    finish(xlink())

    def widen_rows(z, carry):
        vf[z + 1, 0:SUB] = xlo[z].astype(F32)[PACK - SUB:]
        vf[z + 1, SUB + xdev:] = xhi[z].astype(F32)[:SUB]
        return carry

    lax.fori_loop(0, zdev, widen_rows, 0, unroll=8)
    def ready(turn):
        place = at_turn(turn)
        rows = rows_of(place)
        body = pl.ds(pl.multiple_of(place * unit + SUB, SUB), unit)
        finish(zlink(place))
        vf[0, body] = zlo[rows].astype(F32)
        vf[zdev + 1, body] = zhi[rows].astype(F32)
        finish(ylink(place))
        mine = face[rows].astype(F32)
        low = pltpu.roll(mine - flo[rows].astype(F32), 1, 1)
        high = pltpu.roll(fhi[rows].astype(F32) - mine, ydev - 1, 1)
        edges[rows] = jnp.where(iota((unit, ydev), 1) % 2 == 0, high, low)

    ready(0)
    patch(0, zdev, row_of(0))

    def tile_turn(turn):
        place = at_turn(turn)
        for sub in range(owners):
            owner = place * owners + sub
            part = pl.ds(sub * rows_out, rows_out)

            @pl.when(owner == me)
            def _():
                own[...] = stage[:, part]

            @pl.when(owner != me)
            def _():
                line = iota((PACK, ydev), 0)
                powers = jnp.zeros((PACK, ydev), F32)
                for chan in range(3):
                    value = stage[chan, part]
                    peak = jnp.maximum(jnp.max(value, axis=0, keepdims=True), 1e-30)
                    power = jnp.ceil(jnp.log2(peak * (1.0 / LEVELS)))
                    powers = jnp.where(line == chan, power, powers)
                    level = (value * jnp.exp2(-power) + 0.5).astype(jnp.int32)
                    tiles_out[owner, chan * plane:chan * plane + rows_out] = level.astype(jnp.int16)
                tiles_out[owner, 3 * plane:] = powers.astype(jnp.int32).astype(jnp.int16)
                tile_copy(owner, me).start()

    def step(at, carry):
        turn = at // per_unit
        final = at % per_unit == per_unit - 1

        @pl.when(final & (turn < units - 1))
        def _():
            ready(turn + 1)

        block(at)

        @pl.when(final)
        def _():
            tile_turn(turn)

        return carry

    lax.fori_loop(0, blocks, step, 0)

    logs_in[me] = logs[pl.ds(pl.multiple_of(me * rows_out, SUB), rows_out)]
    mark = flag[pl.ds(pl.multiple_of(me * rows_out, SUB), rows_out)] > 0.5
    zero = jnp.zeros((rows_out, ydev), F32)
    done, through, total = [zero] * 3, zero + 1.0, zero
    for slab in range(ndepth):
        @pl.when(me != slab)
        def _():
            log_copy(slab, slab).wait()
            tile_copy(slab, slab).wait()

        logt = logs_in[slab]
        clear = jnp.exp(logt)
        keep = jnp.where(mark, clear, 1.0)
        ahead = jnp.where(mark, 1.0, through)
        powers = jnp.exp2(tiles_in[slab, 3 * plane:].astype(jnp.int32).astype(F32))
        for chan in range(3):
            level = tiles_in[slab, chan * plane:chan * plane + rows_out].astype(jnp.int32).astype(F32)
            value = jnp.where(me == slab, own[chan], level * powers[chan:chan + 1])
            done[chan] = keep * done[chan] + ahead * value
        through = through * clear
        total = total + logt
    for chan in range(3):
        colour_out[chan] = done[chan]
    logt_out[...] = total


def hand_over(colour, logt, colour_out, logt_out, sem):
    copies = [pltpu.make_async_copy(src, dst, sem.at[at])
              for at, (src, dst) in enumerate(((colour, colour_out), (logt, logt_out)))]
    for copy in copies:
        copy.start()
    for copy in copies:
        copy.wait()


def local(field, brick_live, order, centers, widths, heights, colours):
    counts = tuple(lax.axis_size(axis) for axis in ("depth", "imx", "imy"))
    zdev, xdev, ydev = field.shape
    ndepth = counts[0]
    rows_out = xdev // ndepth
    step_len = OPTICAL / (zdev * ndepth)
    unit = max(PACK, rows_out)
    units = xdev // unit
    vmem = pl.BlockSpec(memory_space=pltpu.VMEM)
    dma = pltpu.SemaphoreType.DMA
    done = pl.pallas_call(
        functools.partial(kernel, counts, step_len),
        out_shape=(
            pltpu.VMEM((3, rows_out, ydev), F32),
            pltpu.VMEM((rows_out, ydev), F32),
        ),
        in_specs=[pl.BlockSpec(memory_space=pl.ANY)] * 7,
        out_specs=(vmem, vmem),
        scratch_shapes=[
            pltpu.VMEM((zdev, xdev, ydev), BF16),
            pltpu.VMEM(brick_live.shape, jnp.int32),
            pltpu.VMEM(order.shape, jnp.int32),
            pltpu.SMEM(centers.shape, F32),
            pltpu.SMEM(widths.shape, F32),
            pltpu.SMEM(heights.shape, F32),
            pltpu.SMEM(colours.shape, F32),
            pltpu.VMEM((zdev + 2, xdev + 2 * SUB, ydev), F32),
            pltpu.VMEM((xdev, ydev), BF16),
            pltpu.VMEM((xdev, ydev), BF16),
            pltpu.VMEM((zdev, PACK, ydev), BF16),
            pltpu.VMEM((zdev, PACK, ydev), BF16),
            pltpu.VMEM((xdev, ydev), BF16),
            pltpu.VMEM((xdev, ydev), BF16),
            pltpu.VMEM((xdev, ydev), BF16),
            pltpu.VMEM((xdev, ydev), F32),
            pltpu.VMEM((zdev, xdev, ydev), F32),
            pltpu.VMEM((3, centers.shape[0], PACK, ydev), F32),
            pltpu.VMEM((zdev, xdev, ydev), F32),
            pltpu.VMEM((centers.shape[0], zdev, xdev, ydev), F32),
            pltpu.VMEM((xdev, ydev), F32),
            pltpu.VMEM((xdev, ydev), F32),
            pltpu.VMEM((xdev, ydev), F32),
            pltpu.VMEM((ndepth, rows_out, ydev), F32),
            pltpu.VMEM((ndepth, 3 * max(PACK, rows_out) + PACK, ydev), jnp.int16),
            pltpu.VMEM((ndepth, 3 * max(PACK, rows_out) + PACK, ydev), jnp.int16),
            pltpu.VMEM((3, unit, ydev), F32),
            pltpu.VMEM((3, rows_out, ydev), F32),
            dma((6,)),
            dma((PIECES,)),
            dma((4 * units + 2,)),
            dma((4 * units + 2,)),
            dma((ndepth,)),
            dma((ndepth,)),
            dma((ndepth,)),
            dma((ndepth,)),
        ],
        compiler_params=pltpu.CompilerParams(
            collective_id=0, has_side_effects=True),
    )(field, brick_live, order, centers, widths, heights, colours)
    return pl.pallas_call(
        hand_over,
        out_shape=tuple(jax.ShapeDtypeStruct(part.shape, F32) for part in done),
        in_specs=[vmem] * 2,
        out_specs=(pl.BlockSpec(memory_space=pl.ANY),) * 2,
        scratch_shapes=[dma((2,))],
    )(*(pltpu.with_memory_space_constraint(part, pltpu.VMEM) for part in done))


def solution(mesh):
    return jax.shard_map(
        local,
        mesh=mesh,
        in_specs=(
            P("depth", "imy", "imx"),
            P("depth", "imy", "imx"),
            P("imy", "imx"),
            P(),
            P(),
            P(),
            P(),
        ),
        out_specs=(P(None, ("imy", "depth"), "imx"), P(("imy", "depth"), "imx")),
        check_vma=False,
    )
```

```python
import functools
import math

import jax
import jax.numpy as jnp
from jax import lax
from jax.experimental import pallas as pl
from jax.experimental.pallas import tpu as pltpu
from jax.sharding import PartitionSpec as P

OPTICAL = 3.0
MESH = pl.DeviceIdType.MESH
SUB = 8
PACK = 16
F32 = jnp.float32
BF16 = jnp.bfloat16
LEVELS = 32000.0
UNROLL_A = 16
CHUNK = 16
PIECES = 2
EARLY = 0
LOG2E = math.log2(math.e)


def iota(shape, dim):
    return lax.broadcasted_iota(jnp.int32, shape, dim)


def expand(small, rows, cols):
    high, wide = small.shape
    along = (iota((wide, cols), 1) // (cols // wide) == iota((wide, cols), 0)).astype(F32).astype(BF16)
    tall = jnp.dot(small.astype(F32).astype(BF16), along, preferred_element_type=F32)
    return jnp.broadcast_to(tall[:, None, :], (high, rows // high, cols)).reshape(rows, cols)


def kernel(
    counts, step_len,
    field, live_in, order_in, centers_in, widths_in, heights_in, colours_in,
    colour_out, logt_out,
    fb, live, order, centers, widths, heights, colours,
    vf, zlo, zhi, xlo, xhi, face, flo, fhi, edges, slopes, splats, weights, lobes, scales, flag, logs, logs_in,
    tiles_out, tiles_in, stage, own,
    load_sem, piece_sem, halo_send, halo_recv, log_send, log_recv, tile_send, tile_recv,
):
    ndepth, nimx, nimy = counts
    me = lax.axis_index("depth")
    mx = lax.axis_index("imx")
    my = lax.axis_index("imy")
    zdev, xdev, ydev = fb.shape
    rows_out = xdev // ndepth
    nb = centers.shape[0]
    unit = max(PACK, rows_out)
    units, per_unit, owners = xdev // unit, unit // PACK, unit // rows_out
    blocks = units * per_unit
    span = zdev // PIECES
    early = jnp.clip(ndepth - 1 - 2 * me, 0, min(EARLY, units))
    plane = max(PACK, rows_out)

    def at_turn(turn):
        if owners > 1:
            return turn
        return jnp.where(turn < me, turn, ndepth - 1 - turn + me)

    def rows_of(place):
        return pl.ds(pl.multiple_of(place * unit, PACK), unit)

    def piece_load(piece):
        part = pl.ds(piece * span, span)
        return pltpu.make_async_copy(field.at[part], fb.at[part], piece_sem.at[piece])

    barrier = pltpu.get_barrier_semaphore()
    for axis, pos, count in (("imx", mx, nimx), ("imy", my, nimy)):
        @pl.when(pos > 0)
        def _():
            pl.semaphore_signal(barrier, inc=1, device_id={axis: pos - 1}, device_id_type=MESH)

        @pl.when(pos < count - 1)
        def _():
            pl.semaphore_signal(barrier, inc=1, device_id={axis: pos + 1}, device_id_type=MESH)

    for step in range(1, ndepth):
        pl.semaphore_signal(barrier, inc=1, device_id={"depth": lax.rem(me + step, ndepth)}, device_id_type=MESH)

    pairs = ((order_in, order), (live_in, live), (centers_in, centers),
             (widths_in, widths), (heights_in, heights), (colours_in, colours))
    loads = [pltpu.make_async_copy(src, dst, load_sem.at[at]) for at, (src, dst) in enumerate(pairs)]
    for load in loads:
        load.start()
    for piece in range(PIECES):
        piece_load(piece).start()

    for pos, count, low, high in ((me, ndepth, zlo, zhi), (mx, nimx, flo, fhi), (my, nimy, xlo, xhi)):
        @pl.when(pos == 0)
        def _():
            low[...] = jnp.zeros(low.shape, BF16)

        @pl.when(pos == count - 1)
        def _():
            high[...] = jnp.zeros(high.shape, BF16)

    def links(axis, pos, count, down_src, up_src, low, high, at):
        to_low = pltpu.make_async_remote_copy(
            src_ref=down_src, dst_ref=high, send_sem=halo_send.at[at], recv_sem=halo_recv.at[at],
            device_id={axis: lax.rem(pos + count - 1, count)}, device_id_type=MESH)
        to_high = pltpu.make_async_remote_copy(
            src_ref=up_src, dst_ref=low, send_sem=halo_send.at[at + 1], recv_sem=halo_recv.at[at + 1],
            device_id={axis: lax.rem(pos + 1, count)}, device_id_type=MESH)
        return pos, count, to_low, to_high

    def start(link):
        pos, count, to_low, to_high = link

        @pl.when(pos > 0)
        def _():
            to_low.start()

        @pl.when(pos < count - 1)
        def _():
            to_high.start()

    def finish(link):
        pos, count, to_low, to_high = link

        @pl.when(pos > 0)
        def _():
            to_low.wait_send()
            to_high.wait_recv()

        @pl.when(pos < count - 1)
        def _():
            to_high.wait_send()
            to_low.wait_recv()

    def zlink(place):
        rows = rows_of(place)
        return links("depth", me, ndepth, field.at[0, rows], field.at[zdev - 1, rows], zlo.at[rows], zhi.at[rows], 2 * place)

    def ylink(place):
        rows = rows_of(place)
        return links("imx", mx, nimx, face.at[rows], face.at[rows], flo.at[rows], fhi.at[rows], 2 * units + 2 * place)

    def xlink():
        return links("imy", my, nimy, field.at[:, pl.ds(0, PACK)], field.at[:, pl.ds(xdev - PACK, PACK)], xlo, xhi, 4 * units)

    for load in loads:
        load.wait()
    back = expand(order[...], xdev, ydev)
    factor = (2.0 * back - 1.0) * expand(live[0], xdev, ydev) * (step_len * LOG2E)
    flag[...] = back
    scales[...] = factor
    for j in range(nb):
        wid = jnp.full((PACK, ydev), widths[j], F32)
        splats[0, j] = jnp.full((PACK, ydev), centers[j], F32)
        splats[1, j] = (-0.5 * LOG2E) / (wid * wid)
    lane = iota((PACK, ydev), 1)

    def absorb(row):
        here = pl.ds(pl.multiple_of(row, PACK), PACK)
        body = pl.ds(pl.multiple_of(row + SUB, SUB), PACK)
        fac = scales[here]
        for j in range(nb):
            splats[2, j] = heights[j] * fac

        def sample(z, carry):
            depth, gone = carry
            val = fb[z, here].astype(F32)
            vf[z + 1, body] = val
            terms = []
            for j in range(nb):
                off = val - splats[0, j]
                if j == 0:
                    slopes[z, here] = pltpu.roll(off, ydev - 1, 1) - pltpu.roll(off, 1, 1)
                bump = jnp.exp2(off * splats[1, j] * off)
                lobes[j, z, here] = bump
                terms.append(splats[2, j] * bump)
            while len(terms) > 1:
                terms = [sum(terms[at:at + 2][1:], terms[at]) for at in range(0, len(terms), 2)]
            depth = depth + terms[0]
            now = jnp.exp2(depth)
            weights[z, here] = now - gone
            return depth, now

        zero = jnp.zeros((PACK, ydev), F32)
        depth, _ = lax.fori_loop(0, zdev, sample, (zero, zero + 1.0), unroll=UNROLL_A)
        mark = flag[here] > 0.5
        scales[here] = jnp.where(mark, jnp.exp2(-depth), -1.0)
        logs[here] = jnp.where(mark, -depth, depth) * (1.0 / LOG2E)

    def log_copy(owner, source):
        return pltpu.make_async_remote_copy(
            src_ref=logs.at[pl.ds(pl.multiple_of(owner * rows_out, SUB), rows_out)], dst_ref=logs_in.at[source],
            send_sem=log_send.at[owner], recv_sem=log_recv.at[source], device_id={"depth": owner}, device_id_type=MESH)

    def send_logs(turn, carry):
        for sub in range(owners):
            owner = at_turn(turn) * owners + sub

            @pl.when(owner != me)
            def _():
                log_copy(owner, me).start()

        return carry

    def absorb_turn(turn, carry):
        place = at_turn(turn)

        def one(i, inside):
            absorb(place * unit + i * PACK)
            return inside

        return lax.fori_loop(0, per_unit, one, carry)

    wide = iota((xdev, ydev), 1) // 2
    packed = jnp.zeros((xdev, ydev), BF16)
    for piece in range(PIECES):
        piece_load(piece).wait()
        for z in range(piece * span, piece * span + span):
            packed = jnp.where(wide == z, pltpu.roll(fb[z], 2 * z + 1, 1), packed)
    face[...] = packed

    if EARLY:
        lax.fori_loop(0, early, absorb_turn, 0)
    peers = ndepth - 1
    for pos, count in ((mx, nimx), (my, nimy)):
        peers = peers + (pos + count - 1) // count + (2 * count - 2 - pos) // count
    pl.semaphore_wait(barrier, peers)

    def start_turn(turn, carry):
        start(zlink(at_turn(turn)))
        start(ylink(at_turn(turn)))
        return carry

    start_turn(0, 0)
    start(xlink())
    lax.fori_loop(1, units, start_turn, 0)
    if EARLY:
        lax.fori_loop(0, early, send_logs, 0)

    def next_turn(turn, carry):
        absorb_turn(turn, carry)
        return send_logs(turn, carry)

    lax.fori_loop(early if EARLY else 0, units, next_turn, 0)

    outermost = (lane == 0) | (lane == ydev - 1)

    def row_of(at):
        return at_turn(at // per_unit) * unit + at % per_unit * PACK

    def patch(first, count, row):
        here = pl.ds(pl.multiple_of(row, PACK), PACK)
        outer = edges[here]
        for z in range(count):
            edge = pltpu.roll(outer, ydev - 1 - 2 * (first + z), 1)
            pltpu.store(slopes.at[first + z, here], slopes[first + z, here] + edge, mask=outermost)

    def block(at):
        row = row_of(at)
        following = row_of(jnp.minimum(at + 1, blocks - 1))
        here = pl.ds(pl.multiple_of(row, PACK), PACK)
        body = pl.ds(pl.multiple_of(row + SUB, SUB), PACK)
        above = pl.ds(row + SUB - 1, PACK)
        below = pl.ds(row + SUB + 1, PACK)

        def chunk(c, carry):
            prev, val, sums = carry
            for i in range(CHUNK):
                z = c * CHUNK + i
                after = vf[z + 2, body]
                dz = after - prev
                dx = vf[z + 1, below] - vf[z + 1, above]
                dy = slopes[z, here]
                facing = (0.7 * 0.64) * dz + (0.7 * 0.48) * dx + (0.7 * 0.6) * dy
                shade = 0.3 + jnp.abs(facing) * lax.rsqrt(dz * dz + dx * dx + dy * dy + 4.0)
                weight = weights[z, here] * shade.astype(BF16).astype(F32)
                sums = tuple(acc + weight * lobes[j, z, here] for j, acc in enumerate(sums))
                prev, val = val, after
            patch(c * CHUNK, CHUNK, following)
            return prev, val, sums

        zero = jnp.zeros((PACK, ydev), F32)
        init = (vf[0, body], vf[1, body], (zero,) * nb)
        _, _, sums = lax.fori_loop(0, zdev // CHUNK, chunk, init)
        scale = scales[here]
        spot = pl.ds(pl.multiple_of(at % per_unit * PACK, PACK), PACK)
        for chan in range(3):
            total = None
            for j in range(nb):
                term = colours[j, chan] * sums[j]
                total = term if total is None else total + term
            stage[chan, spot] = total * scale

    def tile_copy(owner, source):
        return pltpu.make_async_remote_copy(
            src_ref=tiles_out.at[owner], dst_ref=tiles_in.at[source], send_sem=tile_send.at[owner],
            recv_sem=tile_recv.at[source], device_id={"depth": owner}, device_id_type=MESH)

    tiles_in[me] = jnp.zeros(tiles_in.shape[1:], jnp.int16)
    finish(xlink())

    def widen_rows(z, carry):
        vf[z + 1, 0:SUB] = xlo[z].astype(F32)[PACK - SUB:]
        vf[z + 1, SUB + xdev:] = xhi[z].astype(F32)[:SUB]
        return carry

    lax.fori_loop(0, zdev, widen_rows, 0, unroll=8)
    def ready(turn):
        place = at_turn(turn)
        rows = rows_of(place)
        body = pl.ds(pl.multiple_of(place * unit + SUB, SUB), unit)
        finish(zlink(place))
        vf[0, body] = zlo[rows].astype(F32)
        vf[zdev + 1, body] = zhi[rows].astype(F32)
        finish(ylink(place))
        mine = face[rows].astype(F32)
        low = pltpu.roll(mine - flo[rows].astype(F32), 1, 1)
        high = pltpu.roll(fhi[rows].astype(F32) - mine, ydev - 1, 1)
        edges[rows] = jnp.where(iota((unit, ydev), 1) % 2 == 0, high, low)

    ready(0)
    patch(0, zdev, row_of(0))

    def tile_turn(turn):
        place = at_turn(turn)
        for sub in range(owners):
            owner = place * owners + sub
            part = pl.ds(sub * rows_out, rows_out)

            @pl.when(owner == me)
            def _():
                own[...] = stage[:, part]

            @pl.when(owner != me)
            def _():
                line = iota((PACK, ydev), 0)
                powers = jnp.zeros((PACK, ydev), F32)
                for chan in range(3):
                    value = stage[chan, part]
                    peak = jnp.maximum(jnp.max(value, axis=0, keepdims=True), 1e-30)
                    power = jnp.ceil(jnp.log2(peak * (1.0 / LEVELS)))
                    powers = jnp.where(line == chan, power, powers)
                    level = (value * jnp.exp2(-power) + 0.5).astype(jnp.int32)
                    tiles_out[owner, chan * plane:chan * plane + rows_out] = level.astype(jnp.int16)
                tiles_out[owner, 3 * plane:] = powers.astype(jnp.int32).astype(jnp.int16)
                tile_copy(owner, me).start()

    def step(at, carry):
        turn = at // per_unit
        final = at % per_unit == per_unit - 1

        @pl.when(final & (turn < units - 1))
        def _():
            ready(turn + 1)

        block(at)

        @pl.when(final)
        def _():
            tile_turn(turn)

        return carry

    lax.fori_loop(0, blocks, step, 0)

    logs_in[me] = logs[pl.ds(pl.multiple_of(me * rows_out, SUB), rows_out)]
    mark = flag[pl.ds(pl.multiple_of(me * rows_out, SUB), rows_out)] > 0.5
    zero = jnp.zeros((rows_out, ydev), F32)
    done, through, total = [zero] * 3, zero + 1.0, zero
    for slab in range(ndepth):
        @pl.when(me != slab)
        def _():
            log_copy(slab, slab).wait()
            tile_copy(slab, slab).wait()

        logt = logs_in[slab]
        clear = jnp.exp(logt)
        keep = jnp.where(mark, clear, 1.0)
        ahead = jnp.where(mark, 1.0, through)
        powers = jnp.exp2(tiles_in[slab, 3 * plane:].astype(jnp.int32).astype(F32))
        for chan in range(3):
            level = tiles_in[slab, chan * plane:chan * plane + rows_out].astype(jnp.int32).astype(F32)
            value = jnp.where(me == slab, own[chan], level * powers[chan:chan + 1])
            done[chan] = keep * done[chan] + ahead * value
        through = through * clear
        total = total + logt
    for chan in range(3):
        colour_out[chan] = done[chan]
    logt_out[...] = total


def hand_over(colour, logt, colour_out, logt_out, sem):
    copies = [pltpu.make_async_copy(src, dst, sem.at[at])
              for at, (src, dst) in enumerate(((colour, colour_out), (logt, logt_out)))]
    for copy in copies:
        copy.start()
    for copy in copies:
        copy.wait()


def local(field, brick_live, order, centers, widths, heights, colours):
    counts = tuple(lax.axis_size(axis) for axis in ("depth", "imx", "imy"))
    zdev, xdev, ydev = field.shape
    ndepth = counts[0]
    rows_out = xdev // ndepth
    step_len = OPTICAL / (zdev * ndepth)
    unit = max(PACK, rows_out)
    units = xdev // unit
    vmem = pl.BlockSpec(memory_space=pltpu.VMEM)
    dma = pltpu.SemaphoreType.DMA
    done = pl.pallas_call(
        functools.partial(kernel, counts, step_len),
        out_shape=(
            pltpu.VMEM((3, rows_out, ydev), F32),
            pltpu.VMEM((rows_out, ydev), F32),
        ),
        in_specs=[pl.BlockSpec(memory_space=pl.ANY)] * 7,
        out_specs=(vmem, vmem),
        scratch_shapes=[
            pltpu.VMEM((zdev, xdev, ydev), BF16),
            pltpu.VMEM(brick_live.shape, jnp.int32),
            pltpu.VMEM(order.shape, jnp.int32),
            pltpu.SMEM(centers.shape, F32),
            pltpu.SMEM(widths.shape, F32),
            pltpu.SMEM(heights.shape, F32),
            pltpu.SMEM(colours.shape, F32),
            pltpu.VMEM((zdev + 2, xdev + 2 * SUB, ydev), F32),
            pltpu.VMEM((xdev, ydev), BF16),
            pltpu.VMEM((xdev, ydev), BF16),
            pltpu.VMEM((zdev, PACK, ydev), BF16),
            pltpu.VMEM((zdev, PACK, ydev), BF16),
            pltpu.VMEM((xdev, ydev), BF16),
            pltpu.VMEM((xdev, ydev), BF16),
            pltpu.VMEM((xdev, ydev), BF16),
            pltpu.VMEM((xdev, ydev), F32),
            pltpu.VMEM((zdev, xdev, ydev), F32),
            pltpu.VMEM((3, centers.shape[0], PACK, ydev), F32),
            pltpu.VMEM((zdev, xdev, ydev), F32),
            pltpu.VMEM((centers.shape[0], zdev, xdev, ydev), F32),
            pltpu.VMEM((xdev, ydev), F32),
            pltpu.VMEM((xdev, ydev), F32),
            pltpu.VMEM((xdev, ydev), F32),
            pltpu.VMEM((ndepth, rows_out, ydev), F32),
            pltpu.VMEM((ndepth, 3 * max(PACK, rows_out) + PACK, ydev), jnp.int16),
            pltpu.VMEM((ndepth, 3 * max(PACK, rows_out) + PACK, ydev), jnp.int16),
            pltpu.VMEM((3, unit, ydev), F32),
            pltpu.VMEM((3, rows_out, ydev), F32),
            dma((6,)),
            dma((PIECES,)),
            dma((4 * units + 2,)),
            dma((4 * units + 2,)),
            dma((ndepth,)),
            dma((ndepth,)),
            dma((ndepth,)),
            dma((ndepth,)),
        ],
        compiler_params=pltpu.CompilerParams(
            collective_id=0, has_side_effects=True),
    )(field, brick_live, order, centers, widths, heights, colours)
    return pl.pallas_call(
        hand_over,
        out_shape=tuple(jax.ShapeDtypeStruct(part.shape, F32) for part in done),
        in_specs=[vmem] * 2,
        out_specs=(pl.BlockSpec(memory_space=pl.ANY),) * 2,
        scratch_shapes=[dma((2,))],
    )(*(pltpu.with_memory_space_constraint(part, pltpu.VMEM) for part in done))


def solution(mesh):
    return jax.shard_map(
        local,
        mesh=mesh,
        in_specs=(
            P("depth", "imy", "imx"),
            P("depth", "imy", "imx"),
            P("imy", "imx"),
            P(),
            P(),
            P(),
            P(),
        ),
        out_specs=(P(None, ("imy", "depth"), "imx"), P(("imy", "depth"), "imx")),
        check_vma=False,
    )
```

```python
import functools
import math

import jax
import jax.numpy as jnp
from jax import lax
from jax.experimental import pallas as pl
from jax.experimental.pallas import tpu as pltpu
from jax.sharding import PartitionSpec as P

OPTICAL = 3.0
MESH = pl.DeviceIdType.MESH
SUB = 8
PACK = 16
F32 = jnp.float32
BF16 = jnp.bfloat16
LEVELS = 32000.0
UNROLL_A = 16
CHUNK = 16
PIECES = 1
EARLY = 0
LOG2E = math.log2(math.e)


def iota(shape, dim):
    return lax.broadcasted_iota(jnp.int32, shape, dim)


def expand(small, rows, cols):
    high, wide = small.shape
    along = (iota((wide, cols), 1) // (cols // wide) == iota((wide, cols), 0)).astype(F32).astype(BF16)
    tall = jnp.dot(small.astype(F32).astype(BF16), along, preferred_element_type=F32)
    return jnp.broadcast_to(tall[:, None, :], (high, rows // high, cols)).reshape(rows, cols)


def kernel(
    counts, step_len,
    field, live_in, order_in, centers_in, widths_in, heights_in, colours_in,
    colour_out, logt_out,
    fb, live, order, centers, widths, heights, colours,
    vf, zlo, zhi, xlo, xhi, face, flo, fhi, edges, slopes, splats, weights, lobes, scales, flag, logs, logs_in,
    tiles_out, tiles_in, stage, own,
    load_sem, piece_sem, halo_send, halo_recv, log_send, log_recv, tile_send, tile_recv,
):
    ndepth, nimx, nimy = counts
    me = lax.axis_index("depth")
    mx = lax.axis_index("imx")
    my = lax.axis_index("imy")
    zdev, xdev, ydev = fb.shape
    rows_out = xdev // ndepth
    nb = centers.shape[0]
    unit = max(PACK, rows_out)
    units, per_unit, owners = xdev // unit, unit // PACK, unit // rows_out
    blocks = units * per_unit
    span = zdev // PIECES
    early = jnp.clip(ndepth - 1 - 2 * me, 0, min(EARLY, units))
    plane = max(PACK, rows_out)

    def at_turn(turn):
        if owners > 1:
            return turn
        return jnp.where(turn < me, turn, ndepth - 1 - turn + me)

    def rows_of(place):
        return pl.ds(pl.multiple_of(place * unit, PACK), unit)

    def piece_load(piece):
        part = pl.ds(piece * span, span)
        return pltpu.make_async_copy(field.at[part], fb.at[part], piece_sem.at[piece])

    barrier = pltpu.get_barrier_semaphore()
    for axis, pos, count in (("imx", mx, nimx), ("imy", my, nimy)):
        @pl.when(pos > 0)
        def _():
            pl.semaphore_signal(barrier, inc=1, device_id={axis: pos - 1}, device_id_type=MESH)

        @pl.when(pos < count - 1)
        def _():
            pl.semaphore_signal(barrier, inc=1, device_id={axis: pos + 1}, device_id_type=MESH)

    for step in range(1, ndepth):
        pl.semaphore_signal(barrier, inc=1, device_id={"depth": lax.rem(me + step, ndepth)}, device_id_type=MESH)

    pairs = ((order_in, order), (live_in, live), (centers_in, centers),
             (widths_in, widths), (heights_in, heights), (colours_in, colours))
    loads = [pltpu.make_async_copy(src, dst, load_sem.at[at]) for at, (src, dst) in enumerate(pairs)]
    for load in loads:
        load.start()
    for piece in range(PIECES):
        piece_load(piece).start()

    for pos, count, low, high in ((me, ndepth, zlo, zhi), (mx, nimx, flo, fhi), (my, nimy, xlo, xhi)):
        @pl.when(pos == 0)
        def _():
            low[...] = jnp.zeros(low.shape, BF16)

        @pl.when(pos == count - 1)
        def _():
            high[...] = jnp.zeros(high.shape, BF16)

    def links(axis, pos, count, down_src, up_src, low, high, at):
        to_low = pltpu.make_async_remote_copy(
            src_ref=down_src, dst_ref=high, send_sem=halo_send.at[at], recv_sem=halo_recv.at[at],
            device_id={axis: lax.rem(pos + count - 1, count)}, device_id_type=MESH)
        to_high = pltpu.make_async_remote_copy(
            src_ref=up_src, dst_ref=low, send_sem=halo_send.at[at + 1], recv_sem=halo_recv.at[at + 1],
            device_id={axis: lax.rem(pos + 1, count)}, device_id_type=MESH)
        return pos, count, to_low, to_high

    def start(link):
        pos, count, to_low, to_high = link

        @pl.when(pos > 0)
        def _():
            to_low.start()

        @pl.when(pos < count - 1)
        def _():
            to_high.start()

    def finish(link):
        pos, count, to_low, to_high = link

        @pl.when(pos > 0)
        def _():
            to_low.wait_send()
            to_high.wait_recv()

        @pl.when(pos < count - 1)
        def _():
            to_high.wait_send()
            to_low.wait_recv()

    def zlink(place):
        rows = rows_of(place)
        return links("depth", me, ndepth, field.at[0, rows], field.at[zdev - 1, rows], zlo.at[rows], zhi.at[rows], 2 * place)

    def ylink(place):
        rows = rows_of(place)
        return links("imx", mx, nimx, face.at[rows], face.at[rows], flo.at[rows], fhi.at[rows], 2 * units + 2 * place)

    def xlink():
        return links("imy", my, nimy, field.at[:, pl.ds(0, PACK)], field.at[:, pl.ds(xdev - PACK, PACK)], xlo, xhi, 4 * units)

    for load in loads:
        load.wait()
    back = expand(order[...], xdev, ydev)
    factor = (2.0 * back - 1.0) * expand(live[0], xdev, ydev) * (step_len * LOG2E)
    flag[...] = back
    scales[...] = factor
    for j in range(nb):
        wid = jnp.full((PACK, ydev), widths[j], F32)
        splats[0, j] = jnp.full((PACK, ydev), centers[j], F32)
        splats[1, j] = (-0.5 * LOG2E) / (wid * wid)
    lane = iota((PACK, ydev), 1)

    def absorb(row):
        here = pl.ds(pl.multiple_of(row, PACK), PACK)
        body = pl.ds(pl.multiple_of(row + SUB, SUB), PACK)
        fac = scales[here]
        for j in range(nb):
            splats[2, j] = heights[j] * fac

        def sample(z, carry):
            depth, gone = carry
            val = fb[z, here].astype(F32)
            vf[z + 1, body] = val
            terms = []
            for j in range(nb):
                off = val - splats[0, j]
                if j == 0:
                    slopes[z, here] = pltpu.roll(off, ydev - 1, 1) - pltpu.roll(off, 1, 1)
                bump = jnp.exp2(off * splats[1, j] * off)
                lobes[j, z, here] = bump
                terms.append(splats[2, j] * bump)
            while len(terms) > 1:
                terms = [sum(terms[at:at + 2][1:], terms[at]) for at in range(0, len(terms), 2)]
            depth = depth + terms[0]
            now = jnp.exp2(depth)
            weights[z, here] = now - gone
            return depth, now

        zero = jnp.zeros((PACK, ydev), F32)
        depth, _ = lax.fori_loop(0, zdev, sample, (zero, zero + 1.0), unroll=UNROLL_A)
        mark = flag[here] > 0.5
        scales[here] = jnp.where(mark, jnp.exp2(-depth), -1.0)
        logs[here] = jnp.where(mark, -depth, depth) * (1.0 / LOG2E)

    def log_copy(owner, source):
        return pltpu.make_async_remote_copy(
            src_ref=logs.at[pl.ds(pl.multiple_of(owner * rows_out, SUB), rows_out)], dst_ref=logs_in.at[source],
            send_sem=log_send.at[owner], recv_sem=log_recv.at[source], device_id={"depth": owner}, device_id_type=MESH)

    def send_logs(turn, carry):
        for sub in range(owners):
            owner = at_turn(turn) * owners + sub

            @pl.when(owner != me)
            def _():
                log_copy(owner, me).start()

        return carry

    def absorb_turn(turn, carry):
        place = at_turn(turn)

        def one(i, inside):
            absorb(place * unit + i * PACK)
            return inside

        return lax.fori_loop(0, per_unit, one, carry)

    wide = iota((xdev, ydev), 1) // 2
    packed = jnp.zeros((xdev, ydev), BF16)
    for piece in range(PIECES):
        piece_load(piece).wait()
        for z in range(piece * span, piece * span + span):
            packed = jnp.where(wide == z, pltpu.roll(fb[z], 2 * z + 1, 1), packed)
    face[...] = packed

    if EARLY:
        lax.fori_loop(0, early, absorb_turn, 0)
    peers = ndepth - 1
    for pos, count in ((mx, nimx), (my, nimy)):
        peers = peers + (pos + count - 1) // count + (2 * count - 2 - pos) // count
    pl.semaphore_wait(barrier, peers)

    def start_turn(turn, carry):
        start(zlink(at_turn(turn)))
        start(ylink(at_turn(turn)))
        return carry

    start_turn(0, 0)
    start(xlink())
    lax.fori_loop(1, units, start_turn, 0)
    if EARLY:
        lax.fori_loop(0, early, send_logs, 0)

    def next_turn(turn, carry):
        absorb_turn(turn, carry)
        return send_logs(turn, carry)

    lax.fori_loop(early if EARLY else 0, units, next_turn, 0)

    outermost = (lane == 0) | (lane == ydev - 1)

    def row_of(at):
        return at_turn(at // per_unit) * unit + at % per_unit * PACK

    def patch(first, count, row):
        here = pl.ds(pl.multiple_of(row, PACK), PACK)
        outer = edges[here]
        for z in range(count):
            edge = pltpu.roll(outer, ydev - 1 - 2 * (first + z), 1)
            pltpu.store(slopes.at[first + z, here], slopes[first + z, here] + edge, mask=outermost)

    def block(at):
        row = row_of(at)
        following = row_of(jnp.minimum(at + 1, blocks - 1))
        here = pl.ds(pl.multiple_of(row, PACK), PACK)
        body = pl.ds(pl.multiple_of(row + SUB, SUB), PACK)
        above = pl.ds(row + SUB - 1, PACK)
        below = pl.ds(row + SUB + 1, PACK)

        def chunk(c, carry):
            prev, val, sums = carry
            for i in range(CHUNK):
                z = c * CHUNK + i
                after = vf[z + 2, body]
                dz = after - prev
                dx = vf[z + 1, below] - vf[z + 1, above]
                dy = slopes[z, here]
                facing = (0.7 * 0.64) * dz + (0.7 * 0.48) * dx + (0.7 * 0.6) * dy
                shade = 0.3 + jnp.abs(facing) * lax.rsqrt(dz * dz + dx * dx + dy * dy + 4.0)
                weight = weights[z, here] * shade.astype(BF16).astype(F32)
                sums = tuple(acc + weight * lobes[j, z, here] for j, acc in enumerate(sums))
                prev, val = val, after
            patch(c * CHUNK, CHUNK, following)
            return prev, val, sums

        zero = jnp.zeros((PACK, ydev), F32)
        init = (vf[0, body], vf[1, body], (zero,) * nb)
        _, _, sums = lax.fori_loop(0, zdev // CHUNK, chunk, init)
        scale = scales[here]
        spot = pl.ds(pl.multiple_of(at % per_unit * PACK, PACK), PACK)
        for chan in range(3):
            total = None
            for j in range(nb):
                term = colours[j, chan] * sums[j]
                total = term if total is None else total + term
            stage[chan, spot] = total * scale

    def tile_copy(owner, source):
        return pltpu.make_async_remote_copy(
            src_ref=tiles_out.at[owner], dst_ref=tiles_in.at[source], send_sem=tile_send.at[owner],
            recv_sem=tile_recv.at[source], device_id={"depth": owner}, device_id_type=MESH)

    tiles_in[me] = jnp.zeros(tiles_in.shape[1:], jnp.int16)
    finish(xlink())

    def widen_rows(z, carry):
        vf[z + 1, 0:SUB] = xlo[z].astype(F32)[PACK - SUB:]
        vf[z + 1, SUB + xdev:] = xhi[z].astype(F32)[:SUB]
        return carry

    lax.fori_loop(0, zdev, widen_rows, 0, unroll=8)
    def ready(turn):
        place = at_turn(turn)
        rows = rows_of(place)
        body = pl.ds(pl.multiple_of(place * unit + SUB, SUB), unit)
        finish(zlink(place))
        vf[0, body] = zlo[rows].astype(F32)
        vf[zdev + 1, body] = zhi[rows].astype(F32)
        finish(ylink(place))
        mine = face[rows].astype(F32)
        low = pltpu.roll(mine - flo[rows].astype(F32), 1, 1)
        high = pltpu.roll(fhi[rows].astype(F32) - mine, ydev - 1, 1)
        edges[rows] = jnp.where(iota((unit, ydev), 1) % 2 == 0, high, low)

    ready(0)
    patch(0, zdev, row_of(0))

    def tile_turn(turn):
        place = at_turn(turn)
        for sub in range(owners):
            owner = place * owners + sub
            part = pl.ds(sub * rows_out, rows_out)

            @pl.when(owner == me)
            def _():
                own[...] = stage[:, part]

            @pl.when(owner != me)
            def _():
                line = iota((PACK, ydev), 0)
                powers = jnp.zeros((PACK, ydev), F32)
                for chan in range(3):
                    value = stage[chan, part]
                    peak = jnp.maximum(jnp.max(value, axis=0, keepdims=True), 1e-30)
                    power = jnp.ceil(jnp.log2(peak * (1.0 / LEVELS)))
                    powers = jnp.where(line == chan, power, powers)
                    level = (value * jnp.exp2(-power) + 0.5).astype(jnp.int32)
                    tiles_out[owner, chan * plane:chan * plane + rows_out] = level.astype(jnp.int16)
                tiles_out[owner, 3 * plane:] = powers.astype(jnp.int32).astype(jnp.int16)
                tile_copy(owner, me).start()

    def step(at, carry):
        turn = at // per_unit
        final = at % per_unit == per_unit - 1

        @pl.when(final & (turn < units - 1))
        def _():
            ready(turn + 1)

        block(at)

        @pl.when(final)
        def _():
            tile_turn(turn)

        return carry

    lax.fori_loop(0, blocks, step, 0)

    logs_in[me] = logs[pl.ds(pl.multiple_of(me * rows_out, SUB), rows_out)]
    mark = flag[pl.ds(pl.multiple_of(me * rows_out, SUB), rows_out)] > 0.5
    zero = jnp.zeros((rows_out, ydev), F32)
    done, through, total = [zero] * 3, zero + 1.0, zero
    for slab in range(ndepth):
        @pl.when(me != slab)
        def _():
            log_copy(slab, slab).wait()
            tile_copy(slab, slab).wait()

        logt = logs_in[slab]
        clear = jnp.exp(logt)
        keep = jnp.where(mark, clear, 1.0)
        ahead = jnp.where(mark, 1.0, through)
        powers = jnp.exp2(tiles_in[slab, 3 * plane:].astype(jnp.int32).astype(F32))
        for chan in range(3):
            level = tiles_in[slab, chan * plane:chan * plane + rows_out].astype(jnp.int32).astype(F32)
            value = jnp.where(me == slab, own[chan], level * powers[chan:chan + 1])
            done[chan] = keep * done[chan] + ahead * value
        through = through * clear
        total = total + logt
    for chan in range(3):
        colour_out[chan] = done[chan]
    logt_out[...] = total


def hand_over(colour, logt, colour_out, logt_out, sem):
    copies = [pltpu.make_async_copy(src, dst, sem.at[at])
              for at, (src, dst) in enumerate(((colour, colour_out), (logt, logt_out)))]
    for copy in copies:
        copy.start()
    for copy in copies:
        copy.wait()


def local(field, brick_live, order, centers, widths, heights, colours):
    counts = tuple(lax.axis_size(axis) for axis in ("depth", "imx", "imy"))
    zdev, xdev, ydev = field.shape
    ndepth = counts[0]
    rows_out = xdev // ndepth
    step_len = OPTICAL / (zdev * ndepth)
    unit = max(PACK, rows_out)
    units = xdev // unit
    vmem = pl.BlockSpec(memory_space=pltpu.VMEM)
    dma = pltpu.SemaphoreType.DMA
    done = pl.pallas_call(
        functools.partial(kernel, counts, step_len),
        out_shape=(
            pltpu.VMEM((3, rows_out, ydev), F32),
            pltpu.VMEM((rows_out, ydev), F32),
        ),
        in_specs=[pl.BlockSpec(memory_space=pl.ANY)] * 7,
        out_specs=(vmem, vmem),
        scratch_shapes=[
            pltpu.VMEM((zdev, xdev, ydev), BF16),
            pltpu.VMEM(brick_live.shape, jnp.int32),
            pltpu.VMEM(order.shape, jnp.int32),
            pltpu.SMEM(centers.shape, F32),
            pltpu.SMEM(widths.shape, F32),
            pltpu.SMEM(heights.shape, F32),
            pltpu.SMEM(colours.shape, F32),
            pltpu.VMEM((zdev + 2, xdev + 2 * SUB, ydev), F32),
            pltpu.VMEM((xdev, ydev), BF16),
            pltpu.VMEM((xdev, ydev), BF16),
            pltpu.VMEM((zdev, PACK, ydev), BF16),
            pltpu.VMEM((zdev, PACK, ydev), BF16),
            pltpu.VMEM((xdev, ydev), BF16),
            pltpu.VMEM((xdev, ydev), BF16),
            pltpu.VMEM((xdev, ydev), BF16),
            pltpu.VMEM((xdev, ydev), F32),
            pltpu.VMEM((zdev, xdev, ydev), F32),
            pltpu.VMEM((3, centers.shape[0], PACK, ydev), F32),
            pltpu.VMEM((zdev, xdev, ydev), F32),
            pltpu.VMEM((centers.shape[0], zdev, xdev, ydev), F32),
            pltpu.VMEM((xdev, ydev), F32),
            pltpu.VMEM((xdev, ydev), F32),
            pltpu.VMEM((xdev, ydev), F32),
            pltpu.VMEM((ndepth, rows_out, ydev), F32),
            pltpu.VMEM((ndepth, 3 * max(PACK, rows_out) + PACK, ydev), jnp.int16),
            pltpu.VMEM((ndepth, 3 * max(PACK, rows_out) + PACK, ydev), jnp.int16),
            pltpu.VMEM((3, unit, ydev), F32),
            pltpu.VMEM((3, rows_out, ydev), F32),
            dma((6,)),
            dma((PIECES,)),
            dma((4 * units + 2,)),
            dma((4 * units + 2,)),
            dma((ndepth,)),
            dma((ndepth,)),
            dma((ndepth,)),
            dma((ndepth,)),
        ],
        compiler_params=pltpu.CompilerParams(
            collective_id=0, has_side_effects=True),
    )(field, brick_live, order, centers, widths, heights, colours)
    return pl.pallas_call(
        hand_over,
        out_shape=tuple(jax.ShapeDtypeStruct(part.shape, F32) for part in done),
        in_specs=[vmem] * 2,
        out_specs=(pl.BlockSpec(memory_space=pl.ANY),) * 2,
        scratch_shapes=[dma((2,))],
    )(*(pltpu.with_memory_space_constraint(part, pltpu.VMEM) for part in done))


def solution(mesh):
    return jax.shard_map(
        local,
        mesh=mesh,
        in_specs=(
            P("depth", "imy", "imx"),
            P("depth", "imy", "imx"),
            P("imy", "imx"),
            P(),
            P(),
            P(),
            P(),
        ),
        out_specs=(P(None, ("imy", "depth"), "imx"), P(("imy", "depth"), "imx")),
        check_vma=False,
    )
```
